256 devices in a mesh: seq: 8 (over x_hi, y), row: 32 (over x_lo, z, core).
Axes of the slice: x: 4 (x_hi: 2, x_lo: 2; x = x_hi * 2 + x_lo), y: 4, z: 8, core: 2. Of those that a mesh axis runs over, the one named last changes fastest.
Arguments:
- tokens: bfloat16 [2, 2048, 3072], P(None, ('seq', 'row')), may hold values from -6 to 6
- w_qkv: bfloat16 [6144, 3072], P('row'), may hold values from -0.109375 to 0.109375
- w_rate: bfloat16 [32, 3072], P('row'), may hold values from -0.109375 to 0.109375
- rate_bias: float32 [32], P('row'), may hold values from -3 to 1
- w_out: bfloat16 [2048, 3072], P('row'), may hold values from -0.125 to 0.125
- w_first_init: float32 [32, 64, 256], P('row'), may hold values from -0.75 to 0.75
- b_first_init: float32 [32, 256], P('row'), may hold values from -3 to 3
- w_second_init: float32 [32, 256, 64], P('row'), may hold values from -0.375 to 0.375
- b_second_init: float32 [32, 64], P('row'), may hold values from -3 to 3
- ln_gain: float32 [32, 64], P('row'), may hold values from 0.5 to 1.5
- ln_bias: float32 [32, 64], P('row'), may hold values from -3 to 3
Outputs:
- mixed: bfloat16 [2, 2048, 3072], P(None, ('seq', 'row'))
The draws below stay inside these ranges and needn't reach their ends.
All inputs are finite; a program needn't handle non-finite values.
Results may differ from the reference program's by a relative error of at most 0.0056.
Values may be sent and summed in bfloat16 or wider, within the bound.
A program may use at most 64 MiB of HBM per device.

```python
import jax
import jax.numpy as jnp
from jax import lax

D = 3072
HEAD_SIZE = 64
INNER = 256
MINI = 64
VIDEOS = 2
HEADS = 32
TOKENS = 2048


def block_scale(own_key, shape, cuts, low, top_value):
    loudness = 1.0
    for axis_at, shards_of in cuts:
        steps = jax.random.uniform(jax.random.fold_in(jax.random.fold_in(own_key, 6), axis_at), (shards_of,), jnp.float32, low / len(cuts), top_value / len(cuts))
        loudness = loudness * jnp.repeat(jnp.exp(steps), shape[axis_at] // shards_of).reshape((-1,) + (1,) * (len(shape) - 1 - axis_at))
    return loudness


def normal_values(stream_key, extent, width, bound, pieces=(), held_as=jnp.bfloat16):
    gain = block_scale(stream_key, extent, pieces, -0.22, 0.18) if pieces else 1.0
    values = jax.random.normal(stream_key, extent, jnp.float32) * width * gain
    return jnp.minimum(jnp.maximum(values, -bound), bound).astype(held_as)


def setup_inputs(seed: int = 0) -> dict:
    arg_keys = jax.random.split(jax.random.key(seed), 12)
    return {
        "tokens": normal_values(arg_keys[0], (VIDEOS, TOKENS, D), 1.0, 6.0, ((1, 256),)),
        "w_qkv": normal_values(arg_keys[1], (HEADS * 3 * HEAD_SIZE, D), D ** -0.5, 0.109375, ((0, 32),)),
        "w_rate": normal_values(arg_keys[2], (HEADS, D), D ** -0.5, 0.109375, ((0, 32),)),
        "rate_bias": jnp.clip(-3.0 + 4.0 * jax.random.uniform(arg_keys[3], (HEADS,), jnp.float32) ** block_scale(arg_keys[3], (HEADS,), ((0, 32),), -0.2, 0.2), -3.0, 1.0),
        "w_out": normal_values(arg_keys[4], (HEADS * HEAD_SIZE, D), (HEADS * HEAD_SIZE) ** -0.5, 0.125, ((0, 32),)),
        "w_first_init": normal_values(arg_keys[5], (HEADS, HEAD_SIZE, INNER), HEAD_SIZE ** -0.5, 0.75, ((0, 32),), jnp.float32),
        "b_first_init": normal_values(arg_keys[6], (HEADS, INNER), 0.5, 3.0, ((0, 32),), jnp.float32),
        "w_second_init": normal_values(arg_keys[7], (HEADS, INNER, HEAD_SIZE), INNER ** -0.5, 0.375, ((0, 32),), jnp.float32),
        "b_second_init": normal_values(arg_keys[8], (HEADS, HEAD_SIZE), 0.5, 3.0, ((0, 32),), jnp.float32),
        "ln_gain": jnp.clip(1.0 + 0.1 * jax.random.normal(arg_keys[9], (HEADS, HEAD_SIZE), jnp.float32), 0.5, 1.5),
        "ln_bias": normal_values(arg_keys[10], (HEADS, HEAD_SIZE), 0.5, 3.0, ((0, 32),), jnp.float32),
    }


gelu_coef = 0.7978845608028654
base_rate = 0.01
ln_eps = 1e-06

def gelu_tanh(entries):
    tanh_arg = gelu_coef * (entries + 0.044715 * entries * entries * entries)
    return 0.5 * entries * (1.0 + jnp.tanh(tanh_arg))

def gelu_slope(entries):
    tanh_arg = gelu_coef * (entries + 0.044715 * entries * entries * entries)
    tangent = jnp.tanh(tanh_arg)
    return 0.5 * (1.0 + tangent) + 0.5 * entries * (1.0 - tangent * tangent) * gelu_coef * (1.0 + 3.0 * 0.044715 * entries * entries)

def matmul(left, right):
    return jnp.dot(left, right, precision=lax.Precision.HIGHEST, preferred_element_type=jnp.float32)

def normalize(entries):
    centred = entries - lax.optimization_barrier(jnp.mean(entries, axis=-1, keepdims=True))
    spread = jnp.sqrt(lax.optimization_barrier(jnp.mean(centred * centred, axis=-1, keepdims=True)) + ln_eps)
    return (centred / spread, spread)

def mini_step(inner_state, batch_block, norm_gain, offset):
    w_first, b_first, w_second, b_second = inner_state
    queries, key_rows, value_rows, lr_rows = batch_block
    mini_len = queries.shape[0]
    hidden_pre = matmul(key_rows, w_first) + b_first
    hidden = gelu_tanh(hidden_pre)
    second = matmul(hidden, w_second) + b_second
    target = value_rows - key_rows
    normed, spread = normalize(second)
    grad_out = norm_gain * (norm_gain * normed + offset - target)
    feat_width = second.shape[-1]
    grad_second = (feat_width * grad_out - lax.optimization_barrier(jnp.sum(grad_out, axis=-1, keepdims=True)) - normed * lax.optimization_barrier(jnp.sum(grad_out * normed, axis=-1, keepdims=True))) / (feat_width * spread)
    grad_first = matmul(grad_second, w_second.T) * gelu_slope(hidden_pre)
    tri_mask = jnp.tril(jnp.ones((mini_len, mini_len), jnp.float32))
    eta_last = lr_rows / mini_len
    eta_table = tri_mask * eta_last[None, :]
    query_keys = matmul(queries, key_rows.T) * eta_table
    bias_first = b_first - matmul(eta_table, grad_first)
    first_bar = matmul(queries, w_first) - matmul(query_keys, grad_first) + bias_first
    hidden_bar = gelu_tanh(first_bar)
    hidden_pairs = matmul(hidden_bar, hidden.T) * eta_table
    bias_second = b_second - matmul(eta_table, grad_second)
    second_bar = matmul(hidden_bar, w_second) - matmul(hidden_pairs, grad_second) + bias_second
    w_first = w_first - matmul((key_rows * eta_last[:, None]).T, grad_first)
    b_first = b_first - matmul(eta_last[None, :], grad_first)[0]
    w_second = w_second - matmul((hidden * eta_last[:, None]).T, grad_second)
    b_second = b_second - matmul(eta_last[None, :], grad_second)[0]
    normed_bar, spread_bar = normalize(second_bar)
    result = queries + norm_gain * normed_bar + offset
    return ((w_first, b_first, w_second, b_second), result)

def run_blocks(inner_state, queries, key_rows, value_rows, lr_rows, norm_gain, offset, mini_len):
    block_count = queries.shape[0] // mini_len
    blocks = (queries.reshape(block_count, mini_len, -1), key_rows.reshape(block_count, mini_len, -1), value_rows.reshape(block_count, mini_len, -1), lr_rows.reshape(block_count, mini_len))

    def advance(loop_carry, batch_block):
        return mini_step(loop_carry, batch_block, norm_gain, offset)
    inner_state, results = lax.scan(advance, inner_state, blocks)
    return (inner_state, results.reshape(queries.shape[0], -1))

def reference(tokens, w_qkv, w_rate, rate_bias, w_out, w_first_init, b_first_init, w_second_init, b_second_init, ln_gain, ln_bias):
    flat_rows = tokens.reshape(-1, D)
    projected = lax.optimization_barrier(jnp.dot(flat_rows, w_qkv.T, preferred_element_type=jnp.float32).astype(jnp.bfloat16)).astype(jnp.float32)
    projected = projected.reshape(VIDEOS, TOKENS, HEADS, 3, HEAD_SIZE).transpose(2, 3, 0, 1, 4)
    lr_all = base_rate * jax.nn.sigmoid(jnp.dot(flat_rows, w_rate.T, preferred_element_type=jnp.float32) + rate_bias)
    lr_all = lr_all.reshape(VIDEOS, TOKENS, HEADS).transpose(2, 0, 1)

    def one_head(w_first, b_first, w_second, b_second, norm_gain, offset, queries, key_rows, value_rows, lr_rows):

        def one_video(video_q, video_k, video_v, video_lr):
            return run_blocks((w_first, b_first, w_second, b_second), video_q, video_k, video_v, video_lr, norm_gain, offset, MINI)[1]
        return jax.vmap(one_video)(queries, key_rows, value_rows, lr_rows)
    heads_all = jax.vmap(one_head)(w_first_init, b_first_init, w_second_init, b_second_init, ln_gain, ln_bias, projected[:, 0], projected[:, 1], projected[:, 2], lr_all)
    heads_out = heads_all.astype(jnp.bfloat16).transpose(1, 2, 0, 3).reshape(VIDEOS * TOKENS, HEADS * HEAD_SIZE)
    mixed = jnp.dot(heads_out, w_out, preferred_element_type=jnp.float32).astype(jnp.bfloat16)
    return mixed.reshape(VIDEOS, TOKENS, D)
```

```python
from functools import partial

import jax
import jax.numpy as jnp
from jax import lax
from jax.sharding import PartitionSpec as P

MINI = 64


gelu_coef = 0.7978845608028654
base_rate = 0.01
ln_eps = 1e-06


def passed_along(array, axis, by):
    size = lax.axis_size(axis)
    pairs = [(i, i + by) for i in range(size) if 0 <= i + by < size]
    return lax.ppermute(array, axis, pairs)


def gelu_tanh(entries):
    tanh_arg = gelu_coef * (entries + 0.044715 * entries * entries * entries)
    return 0.5 * entries * (1.0 + jnp.tanh(tanh_arg))


def gelu_slope(entries):
    tanh_arg = gelu_coef * (entries + 0.044715 * entries * entries * entries)
    tangent = jnp.tanh(tanh_arg)
    return 0.5 * (1.0 + tangent) + 0.5 * entries * (1.0 - tangent * tangent) * gelu_coef * (
        1.0 + 3.0 * 0.044715 * entries * entries
    )


def matmul(left, right):
    return jnp.dot(left, right, precision=lax.Precision.HIGHEST, preferred_element_type=jnp.float32)


def normalize(entries):
    centred = entries - jnp.mean(entries, axis=-1, keepdims=True)
    spread = jnp.sqrt(jnp.mean(centred * centred, axis=-1, keepdims=True) + ln_eps)
    return (centred / spread, spread)


def mini_step(inner_state, batch_block, norm_gain, offset):
    w_first, b_first, w_second, b_second = inner_state
    queries, key_rows, value_rows, lr_rows = batch_block
    mini_len = queries.shape[0]
    hidden_pre = matmul(key_rows, w_first) + b_first
    hidden = gelu_tanh(hidden_pre)
    second = matmul(hidden, w_second) + b_second
    target = value_rows - key_rows
    normed, spread = normalize(second)
    grad_out = norm_gain * (norm_gain * normed + offset - target)
    feat_width = second.shape[-1]
    grad_second = (
        feat_width * grad_out
        - jnp.sum(grad_out, axis=-1, keepdims=True)
        - normed * jnp.sum(grad_out * normed, axis=-1, keepdims=True)
    ) / (feat_width * spread)
    grad_first = matmul(grad_second, w_second.T) * gelu_slope(hidden_pre)
    tri_mask = jnp.tril(jnp.ones((mini_len, mini_len), jnp.float32))
    eta_last = lr_rows / mini_len
    eta_table = tri_mask * eta_last[None, :]
    query_keys = matmul(queries, key_rows.T) * eta_table
    bias_first = b_first - matmul(eta_table, grad_first)
    first_bar = matmul(queries, w_first) - matmul(query_keys, grad_first) + bias_first
    hidden_bar = gelu_tanh(first_bar)
    hidden_pairs = matmul(hidden_bar, hidden.T) * eta_table
    bias_second = b_second - matmul(eta_table, grad_second)
    second_bar = matmul(hidden_bar, w_second) - matmul(hidden_pairs, grad_second) + bias_second
    w_first = w_first - matmul((key_rows * eta_last[:, None]).T, grad_first)
    b_first = b_first - matmul(eta_last[None, :], grad_first)[0]
    w_second = w_second - matmul((hidden * eta_last[:, None]).T, grad_second)
    b_second = b_second - matmul(eta_last[None, :], grad_second)[0]
    normed_bar, spread_bar = normalize(second_bar)
    result = queries + norm_gain * normed_bar + offset
    return ((w_first, b_first, w_second, b_second), result)


def run_blocks(inner_state, queries, key_rows, value_rows, lr_rows, norm_gain, offset, mini_len):
    block_count = queries.shape[0] // mini_len
    blocks = (
        queries.reshape(block_count, mini_len, -1),
        key_rows.reshape(block_count, mini_len, -1),
        value_rows.reshape(block_count, mini_len, -1),
        lr_rows.reshape(block_count, mini_len),
    )

    def advance(loop_carry, batch_block):
        return mini_step(loop_carry, batch_block, norm_gain, offset)

    inner_state, results = lax.scan(advance, inner_state, blocks)
    return (inner_state, results.reshape(queries.shape[0], -1))


def pack_state(state):
    videos = state[0].shape[0]
    return jnp.concatenate([part.reshape(videos, -1) for part in state], axis=1)


def unpack_state(flat, like):
    parts = []
    at = 0
    for part in like:
        width = part[0].size
        parts.append(flat[:, at : at + width].reshape(part.shape))
        at += width
    return tuple(parts)


def on_device(
    tokens,
    w_qkv,
    w_rate,
    rate_bias,
    w_out,
    w_first_init,
    b_first_init,
    w_second_init,
    b_second_init,
    ln_gain,
    ln_bias,
):
    videos, tok_part, feat_width = tokens.shape
    row_axes = ("xlo", "z", "core")
    pair_axes = ("xlo", "core")
    row_count = lax.axis_size(row_axes)
    z_count = lax.axis_size("z")
    pair_count = lax.axis_size(pair_axes)
    seg_len = tok_part * row_count
    proj_width = w_qkv.shape[0]
    head_size = proj_width // 3
    stacked = jnp.concatenate([w_qkv, w_rate], axis=0)
    gathered = lax.all_gather(tokens, row_axes, axis=1, tiled=True)
    gathered, w_out = lax.optimization_barrier((gathered, w_out))
    w_out_pair = lax.all_gather(w_out, pair_axes, axis=0, tiled=True)
    combined = jnp.einsum(
        "vkd,cd->vkc",
        gathered,
        stacked,
        preferred_element_type=jnp.float32,
    )
    projected = lax.optimization_barrier(combined[:, :, :proj_width].astype(jnp.bfloat16)).astype(
        jnp.float32
    )
    queries = projected[:, :, :head_size]
    key_rows = projected[:, :, head_size : 2 * head_size]
    value_rows = projected[:, :, 2 * head_size :]
    lr_rows = base_rate * jax.nn.sigmoid(combined[:, :, proj_width] + rate_bias[0])
    initial = (w_first_init[0], b_first_init[0], w_second_init[0], b_second_init[0])
    norm_gain = ln_gain[0]
    offset = ln_bias[0]

    def segment(inner_state, video_q, video_k, video_v, video_lr):
        return run_blocks(inner_state, video_q, video_k, video_v, video_lr, norm_gain, offset, MINI)

    seq_count = lax.axis_size("seq")
    seq_place = lax.axis_index("seq")
    first_device = seq_place == 0

    def spread_videos(entries):
        return jnp.broadcast_to(entries, (videos,) + entries.shape)

    start_states = jax.tree.map(spread_videos, initial)
    incoming = start_states
    for turn_idx in range(seq_count):
        finals, results = jax.vmap(segment)(incoming, queries, key_rows, value_rows, lr_rows)
        if turn_idx + 1 < seq_count:
            with jax.named_scope("state_hop"):
                received = unpack_state(passed_along(pack_state(finals), "seq", 1), finals)
            incoming = jax.tree.map(partial(jnp.where, first_device), start_states, received)
    heads_rows = results.astype(jnp.bfloat16)
    with jax.named_scope("output_mix"):
        by_owner = heads_rows.reshape(videos, 2, z_count, 2, tok_part, head_size)
        by_owner = by_owner.transpose(1, 3, 0, 2, 4, 5).reshape(
            pair_count, videos, z_count, tok_part, head_size
        )
        by_head = lax.all_to_all(by_owner, pair_axes, 0, 0, tiled=True)
        partial_terms = jnp.einsum(
            "gvzic,gcd->zvid",
            by_head,
            w_out_pair.reshape(pair_count, head_size, feat_width),
            preferred_element_type=jnp.float32,
        )
        mixed_out = lax.psum_scatter(
            partial_terms.reshape(z_count, -1), "z", scatter_dimension=0, tiled=True
        )
        mixed_out = lax.optimization_barrier(mixed_out)
    return mixed_out.reshape(videos, tok_part, feat_width).astype(jnp.bfloat16)


def solution(mesh):
    seq_count, row_count = mesh.devices.shape
    fine = jax.sharding.Mesh(
        mesh.devices.reshape(seq_count, 2, row_count // 4, 2), ("seq", "xlo", "z", "core")
    )
    row = ("xlo", "z", "core")
    in_specs = (
        P(None, ("seq",) + row, None),
        P(row, None),
        P(row, None),
        P(row),
        P(row, None),
        P(row, None, None),
        P(row, None),
        P(row, None, None),
        P(row, None),
        P(row, None),
        P(row, None),
    )
    out_specs = P(None, ("seq",) + row, None)
    return jax.shard_map(
        on_device, mesh=fine, in_specs=in_specs, out_specs=out_specs, check_vma=False
    )
```

```python
from functools import partial

import jax
import jax.numpy as jnp
from jax import lax
from jax.sharding import PartitionSpec as P

MINI = 64


gelu_coef = 0.7978845608028654
base_rate = 0.01
ln_eps = 1e-06


def passed_along(array, axis, by):
    size = lax.axis_size(axis)
    pairs = [(i, i + by) for i in range(size) if 0 <= i + by < size]
    return lax.ppermute(array, axis, pairs)


def gelu_tanh(entries):
    tanh_arg = gelu_coef * (entries + 0.044715 * entries * entries * entries)
    return 0.5 * entries * (1.0 + jnp.tanh(tanh_arg))


def gelu_slope(entries):
    tanh_arg = gelu_coef * (entries + 0.044715 * entries * entries * entries)
    tangent = jnp.tanh(tanh_arg)
    return 0.5 * (1.0 + tangent) + 0.5 * entries * (1.0 - tangent * tangent) * gelu_coef * (
        1.0 + 3.0 * 0.044715 * entries * entries
    )


def matmul(left, right):
    return jnp.dot(left, right, precision=lax.Precision.HIGHEST, preferred_element_type=jnp.float32)


def normalize(entries):
    centred = entries - jnp.mean(entries, axis=-1, keepdims=True)
    spread = jnp.sqrt(jnp.mean(centred * centred, axis=-1, keepdims=True) + ln_eps)
    return (centred / spread, spread)


def mini_step(inner_state, batch_block, norm_gain, offset):
    w_first, b_first, w_second, b_second = inner_state
    queries, key_rows, value_rows, lr_rows = batch_block
    mini_len = queries.shape[0]
    hidden_pre = matmul(key_rows, w_first) + b_first
    hidden = gelu_tanh(hidden_pre)
    second = matmul(hidden, w_second) + b_second
    target = value_rows - key_rows
    normed, spread = normalize(second)
    grad_out = norm_gain * (norm_gain * normed + offset - target)
    feat_width = second.shape[-1]
    grad_second = (
        feat_width * grad_out
        - jnp.sum(grad_out, axis=-1, keepdims=True)
        - normed * jnp.sum(grad_out * normed, axis=-1, keepdims=True)
    ) / (feat_width * spread)
    grad_first = matmul(grad_second, w_second.T) * gelu_slope(hidden_pre)
    tri_mask = jnp.tril(jnp.ones((mini_len, mini_len), jnp.float32))
    eta_last = lr_rows / mini_len
    eta_table = tri_mask * eta_last[None, :]
    query_keys = matmul(queries, key_rows.T) * eta_table
    bias_first = b_first - matmul(eta_table, grad_first)
    first_bar = matmul(queries, w_first) - matmul(query_keys, grad_first) + bias_first
    hidden_bar = gelu_tanh(first_bar)
    hidden_pairs = matmul(hidden_bar, hidden.T) * eta_table
    bias_second = b_second - matmul(eta_table, grad_second)
    second_bar = matmul(hidden_bar, w_second) - matmul(hidden_pairs, grad_second) + bias_second
    w_first = w_first - matmul((key_rows * eta_last[:, None]).T, grad_first)
    b_first = b_first - matmul(eta_last[None, :], grad_first)[0]
    w_second = w_second - matmul((hidden * eta_last[:, None]).T, grad_second)
    b_second = b_second - matmul(eta_last[None, :], grad_second)[0]
    normed_bar, spread_bar = normalize(second_bar)
    result = queries + norm_gain * normed_bar + offset
    return ((w_first, b_first, w_second, b_second), result)


def run_blocks(inner_state, queries, key_rows, value_rows, lr_rows, norm_gain, offset, mini_len):
    block_count = queries.shape[0] // mini_len
    blocks = (
        queries.reshape(block_count, mini_len, -1),
        key_rows.reshape(block_count, mini_len, -1),
        value_rows.reshape(block_count, mini_len, -1),
        lr_rows.reshape(block_count, mini_len),
    )

    def advance(loop_carry, batch_block):
        return mini_step(loop_carry, batch_block, norm_gain, offset)

    inner_state, results = lax.scan(advance, inner_state, blocks)
    return (inner_state, results.reshape(queries.shape[0], -1))


def pack_state(state):
    videos = state[0].shape[0]
    return jnp.concatenate([part.reshape(videos, -1) for part in state], axis=1)


def unpack_state(flat, like):
    parts = []
    at = 0
    for part in like:
        width = part[0].size
        parts.append(flat[:, at : at + width].reshape(part.shape))
        at += width
    return tuple(parts)


def on_device(
    tokens,
    w_qkv,
    w_rate,
    rate_bias,
    w_out,
    w_first_init,
    b_first_init,
    w_second_init,
    b_second_init,
    ln_gain,
    ln_bias,
):
    videos, tok_part, feat_width = tokens.shape
    row_axes = ("xlo", "z", "core")
    pair_axes = ("xlo", "core")
    row_count = lax.axis_size(row_axes)
    z_count = lax.axis_size("z")
    pair_count = lax.axis_size(pair_axes)
    seg_len = tok_part * row_count
    proj_width = w_qkv.shape[0]
    head_size = proj_width // 3
    stacked = jnp.concatenate([w_qkv, w_rate], axis=0)
    gathered = lax.all_gather(tokens, row_axes, axis=1, tiled=True)
    gathered, w_out = lax.optimization_barrier((gathered, w_out))
    w_out_pair = lax.all_gather(w_out, pair_axes, axis=0, tiled=True)
    combined = jnp.einsum(
        "vkd,cd->vkc",
        gathered,
        stacked,
        preferred_element_type=jnp.float32,
    )
    projected = lax.optimization_barrier(combined[:, :, :proj_width].astype(jnp.bfloat16)).astype(
        jnp.float32
    )
    queries = projected[:, :, :head_size]
    key_rows = projected[:, :, head_size : 2 * head_size]
    value_rows = projected[:, :, 2 * head_size :]
    lr_rows = base_rate * jax.nn.sigmoid(combined[:, :, proj_width] + rate_bias[0])
    initial = (w_first_init[0], b_first_init[0], w_second_init[0], b_second_init[0])
    norm_gain = ln_gain[0]
    offset = ln_bias[0]

    def segment(inner_state, video_q, video_k, video_v, video_lr):
        return run_blocks(inner_state, video_q, video_k, video_v, video_lr, norm_gain, offset, MINI)

    seq_count = lax.axis_size("seq")
    seq_place = lax.axis_index("seq")
    first_device = seq_place == 0

    def spread_videos(entries):
        return jnp.broadcast_to(entries, (videos,) + entries.shape)

    start_states = jax.tree.map(spread_videos, initial)
    incoming = start_states
    for turn_idx in range(seq_count):
        finals, results = jax.vmap(segment)(incoming, queries, key_rows, value_rows, lr_rows)
        if turn_idx == 1:
            w_out_pair, finals = lax.optimization_barrier((w_out_pair, finals))
        if turn_idx + 1 < seq_count:
            with jax.named_scope("state_hop"):
                received = unpack_state(passed_along(pack_state(finals), "seq", 1), finals)
            incoming = jax.tree.map(partial(jnp.where, first_device), start_states, received)
    heads_rows = results.astype(jnp.bfloat16)
    with jax.named_scope("output_mix"):
        by_owner = heads_rows.reshape(videos, 2, z_count, 2, tok_part, head_size)
        by_owner = by_owner.transpose(1, 3, 0, 2, 4, 5).reshape(
            pair_count, videos, z_count, tok_part, head_size
        )
        by_head = lax.all_to_all(by_owner, pair_axes, 0, 0, tiled=True)
        partial_terms = jnp.einsum(
            "gvzic,gcd->zvid",
            by_head,
            w_out_pair.reshape(pair_count, head_size, feat_width),
            preferred_element_type=jnp.float32,
        )
        pieces = lax.all_to_all(partial_terms, "z", 0, 0, tiled=True)
        mixed_out = jnp.sum(pieces, axis=0)
    return mixed_out.reshape(videos, tok_part, feat_width).astype(jnp.bfloat16)


def solution(mesh):
    seq_count, row_count = mesh.devices.shape
    fine = jax.sharding.Mesh(
        mesh.devices.reshape(seq_count, 2, row_count // 4, 2), ("seq", "xlo", "z", "core")
    )
    row = ("xlo", "z", "core")
    in_specs = (
        P(None, ("seq",) + row, None),
        P(row, None),
        P(row, None),
        P(row),
        P(row, None),
        P(row, None, None),
        P(row, None),
        P(row, None, None),
        P(row, None),
        P(row, None),
        P(row, None),
    )
    out_specs = P(None, ("seq",) + row, None)
    return jax.shard_map(
        on_device, mesh=fine, in_specs=in_specs, out_specs=out_specs, check_vma=False
    )
```

```python
from functools import partial

import jax
import jax.numpy as jnp
from jax import lax
from jax.experimental import pallas as pl
from jax.experimental.pallas import tpu as pltpu
from jax.sharding import PartitionSpec as P

MESH_ID = pl.DeviceIdType.MESH

MINI = 64


gelu_coef = 0.7978845608028654
base_rate = 0.01
ln_eps = 1e-06


def passed_along(array, axis, by):
    size = lax.axis_size(axis)
    pairs = [(i, i + by) for i in range(size) if 0 <= i + by < size]
    return lax.ppermute(array, axis, pairs)


def gelu_tanh(entries):
    tanh_arg = gelu_coef * (entries + 0.044715 * entries * entries * entries)
    return 0.5 * entries * (1.0 + jnp.tanh(tanh_arg))


def gelu_slope(entries):
    tanh_arg = gelu_coef * (entries + 0.044715 * entries * entries * entries)
    tangent = jnp.tanh(tanh_arg)
    return 0.5 * (1.0 + tangent) + 0.5 * entries * (1.0 - tangent * tangent) * gelu_coef * (
        1.0 + 3.0 * 0.044715 * entries * entries
    )


def matmul(left, right):
    return jnp.dot(left, right, precision=lax.Precision.HIGHEST, preferred_element_type=jnp.float32)


def normalize(entries):
    centred = entries - jnp.mean(entries, axis=-1, keepdims=True)
    spread = jnp.sqrt(jnp.mean(centred * centred, axis=-1, keepdims=True) + ln_eps)
    return (centred / spread, spread)


def mini_step(inner_state, batch_block, norm_gain, offset):
    w_first, b_first, w_second, b_second = inner_state
    queries, key_rows, value_rows, lr_rows = batch_block
    mini_len = queries.shape[0]
    hidden_pre = matmul(key_rows, w_first) + b_first
    hidden = gelu_tanh(hidden_pre)
    second = matmul(hidden, w_second) + b_second
    target = value_rows - key_rows
    normed, spread = normalize(second)
    grad_out = norm_gain * (norm_gain * normed + offset - target)
    feat_width = second.shape[-1]
    grad_second = (
        feat_width * grad_out
        - jnp.sum(grad_out, axis=-1, keepdims=True)
        - normed * jnp.sum(grad_out * normed, axis=-1, keepdims=True)
    ) / (feat_width * spread)
    grad_first = matmul(grad_second, w_second.T) * gelu_slope(hidden_pre)
    tri_mask = jnp.tril(jnp.ones((mini_len, mini_len), jnp.float32))
    eta_last = lr_rows / mini_len
    eta_table = tri_mask * eta_last[None, :]
    query_keys = matmul(queries, key_rows.T) * eta_table
    bias_first = b_first - matmul(eta_table, grad_first)
    first_bar = matmul(queries, w_first) - matmul(query_keys, grad_first) + bias_first
    hidden_bar = gelu_tanh(first_bar)
    hidden_pairs = matmul(hidden_bar, hidden.T) * eta_table
    bias_second = b_second - matmul(eta_table, grad_second)
    second_bar = matmul(hidden_bar, w_second) - matmul(hidden_pairs, grad_second) + bias_second
    w_first = w_first - matmul((key_rows * eta_last[:, None]).T, grad_first)
    b_first = b_first - matmul(eta_last[None, :], grad_first)[0]
    w_second = w_second - matmul((hidden * eta_last[:, None]).T, grad_second)
    b_second = b_second - matmul(eta_last[None, :], grad_second)[0]
    normed_bar, spread_bar = normalize(second_bar)
    result = queries + norm_gain * normed_bar + offset
    return ((w_first, b_first, w_second, b_second), result)


def run_blocks(inner_state, queries, key_rows, value_rows, lr_rows, norm_gain, offset, mini_len):
    block_count = queries.shape[0] // mini_len
    blocks = (
        queries.reshape(block_count, mini_len, -1),
        key_rows.reshape(block_count, mini_len, -1),
        value_rows.reshape(block_count, mini_len, -1),
        lr_rows.reshape(block_count, mini_len),
    )

    def advance(loop_carry, batch_block):
        return mini_step(loop_carry, batch_block, norm_gain, offset)

    inner_state, results = lax.scan(advance, inner_state, blocks)
    return (inner_state, results.reshape(queries.shape[0], -1))


def pack_state(state):
    videos = state[0].shape[0]
    return jnp.concatenate([part.reshape(videos, -1) for part in state], axis=1)


def unpack_state(flat, like):
    parts = []
    at = 0
    for part in like:
        width = part[0].size
        parts.append(flat[:, at : at + width].reshape(part.shape))
        at += width
    return tuple(parts)


def exchange_kernel(peer_count, part_ref, recv_ref, send_sems, recv_sems, own_sem):
    me = lax.axis_index("z")
    barrier = pltpu.get_barrier_semaphore()
    for step in range(1, peer_count):
        peer = lax.rem(me + step, peer_count)
        pl.semaphore_signal(barrier, inc=1, device_id={"z": peer}, device_id_type=MESH_ID)
    pl.semaphore_wait(barrier, peer_count - 1)
    own = pltpu.make_async_copy(part_ref.at[me], recv_ref.at[me], own_sem)
    own.start()
    copies = []
    for step in range(1, peer_count):
        peer = lax.rem(me + step, peer_count)
        copy = pltpu.make_async_remote_copy(
            src_ref=part_ref.at[peer],
            dst_ref=recv_ref.at[me],
            send_sem=send_sems.at[step],
            recv_sem=recv_sems.at[step],
            device_id={"z": peer},
            device_id_type=MESH_ID,
        )
        copy.start()
        copies.append(copy)
    for copy in copies:
        copy.wait()
    own.wait()


def exchange_over_z(pieces):
    peer_count = pieces.shape[0]
    moved = pieces.size * pieces.dtype.itemsize
    return pl.pallas_call(
        partial(exchange_kernel, peer_count),
        out_shape=jax.ShapeDtypeStruct(pieces.shape, pieces.dtype),
        in_specs=[pl.BlockSpec(memory_space=pl.ANY)],
        out_specs=pl.BlockSpec(memory_space=pl.ANY),
        scratch_shapes=[
            pltpu.SemaphoreType.DMA((peer_count,)),
            pltpu.SemaphoreType.DMA((peer_count,)),
            pltpu.SemaphoreType.DMA(()),
        ],
        compiler_params=pltpu.CompilerParams(collective_id=0, has_side_effects=True),
        cost_estimate=pl.CostEstimate(flops=0, bytes_accessed=2 * moved, transcendentals=0),
    )(pieces)


def on_device(
    tokens,
    w_qkv,
    w_rate,
    rate_bias,
    w_out,
    w_first_init,
    b_first_init,
    w_second_init,
    b_second_init,
    ln_gain,
    ln_bias,
):
    videos, tok_part, feat_width = tokens.shape
    row_axes = ("xlo", "z", "core")
    pair_axes = ("xlo", "core")
    row_count = lax.axis_size(row_axes)
    z_count = lax.axis_size("z")
    pair_count = lax.axis_size(pair_axes)
    seg_len = tok_part * row_count
    proj_width = w_qkv.shape[0]
    head_size = proj_width // 3
    stacked = jnp.concatenate([w_qkv, w_rate], axis=0)
    gathered = lax.all_gather(tokens, row_axes, axis=1, tiled=True)
    gathered, w_out = lax.optimization_barrier((gathered, w_out))
    w_out_pair = lax.all_gather(w_out, pair_axes, axis=0, tiled=True)
    combined = jnp.einsum(
        "vkd,cd->vkc",
        gathered,
        stacked,
        preferred_element_type=jnp.float32,
    )
    projected = lax.optimization_barrier(combined[:, :, :proj_width].astype(jnp.bfloat16)).astype(
        jnp.float32
    )
    queries = projected[:, :, :head_size]
    key_rows = projected[:, :, head_size : 2 * head_size]
    value_rows = projected[:, :, 2 * head_size :]
    lr_rows = base_rate * jax.nn.sigmoid(combined[:, :, proj_width] + rate_bias[0])
    initial = (w_first_init[0], b_first_init[0], w_second_init[0], b_second_init[0])
    norm_gain = ln_gain[0]
    offset = ln_bias[0]

    def segment(inner_state, video_q, video_k, video_v, video_lr):
        return run_blocks(inner_state, video_q, video_k, video_v, video_lr, norm_gain, offset, MINI)

    seq_count = lax.axis_size("seq")
    seq_place = lax.axis_index("seq")
    first_device = seq_place == 0

    def spread_videos(entries):
        return jnp.broadcast_to(entries, (videos,) + entries.shape)

    start_states = jax.tree.map(spread_videos, initial)
    incoming = start_states
    for turn_idx in range(seq_count):
        finals, results = jax.vmap(segment)(incoming, queries, key_rows, value_rows, lr_rows)
        if turn_idx == 1:
            w_out_pair, finals = lax.optimization_barrier((w_out_pair, finals))
        if turn_idx + 1 < seq_count:
            with jax.named_scope("state_hop"):
                received = unpack_state(passed_along(pack_state(finals), "seq", 1), finals)
            incoming = jax.tree.map(partial(jnp.where, first_device), start_states, received)
    heads_rows = results.astype(jnp.bfloat16)
    with jax.named_scope("output_mix"):
        by_owner = heads_rows.reshape(videos, 2, z_count, 2, tok_part, head_size)
        by_owner = by_owner.transpose(1, 3, 0, 2, 4, 5).reshape(
            pair_count, videos, z_count, tok_part, head_size
        )
        by_head = lax.all_to_all(by_owner, pair_axes, 0, 0, tiled=True)
        partial_terms = jnp.einsum(
            "gvzic,gcd->zvid",
            by_head,
            w_out_pair.reshape(pair_count, head_size, feat_width),
            preferred_element_type=jnp.float32,
        )
        pieces = exchange_over_z(partial_terms.reshape(z_count, -1))
        mixed_out = jnp.sum(pieces, axis=0)
    return mixed_out.reshape(videos, tok_part, feat_width).astype(jnp.bfloat16)


def solution(mesh):
    seq_count, row_count = mesh.devices.shape
    fine = jax.sharding.Mesh(
        mesh.devices.reshape(seq_count, 2, row_count // 4, 2), ("seq", "xlo", "z", "core")
    )
    row = ("xlo", "z", "core")
    in_specs = (
        P(None, ("seq",) + row, None),
        P(row, None),
        P(row, None),
        P(row),
        P(row, None),
        P(row, None, None),
        P(row, None),
        P(row, None, None),
        P(row, None),
        P(row, None),
        P(row, None),
    )
    out_specs = P(None, ("seq",) + row, None)
    return jax.shard_map(
        on_device, mesh=fine, in_specs=in_specs, out_specs=out_specs, check_vma=False
    )
```

```python
from functools import partial

import jax
import jax.numpy as jnp
from jax import lax
from jax.experimental import pallas as pl
from jax.experimental.pallas import tpu as pltpu
from jax.sharding import PartitionSpec as P

MESH_ID = pl.DeviceIdType.MESH

MINI = 64


gelu_coef = 0.7978845608028654
base_rate = 0.01
ln_eps = 1e-06


def passed_along(array, axis, by):
    size = lax.axis_size(axis)
    pairs = [(i, i + by) for i in range(size) if 0 <= i + by < size]
    return lax.ppermute(array, axis, pairs)


def gelu_tanh(entries):
    tanh_arg = gelu_coef * (entries + 0.044715 * entries * entries * entries)
    return 0.5 * entries * (1.0 + jnp.tanh(tanh_arg))


def gelu_slope(entries):
    tanh_arg = gelu_coef * (entries + 0.044715 * entries * entries * entries)
    tangent = jnp.tanh(tanh_arg)
    return 0.5 * (1.0 + tangent) + 0.5 * entries * (1.0 - tangent * tangent) * gelu_coef * (
        1.0 + 3.0 * 0.044715 * entries * entries
    )


def matmul(left, right):
    return jnp.dot(left, right, precision=lax.Precision.HIGHEST, preferred_element_type=jnp.float32)


def normalize(entries):
    centred = entries - jnp.mean(entries, axis=-1, keepdims=True)
    spread = jnp.sqrt(jnp.mean(centred * centred, axis=-1, keepdims=True) + ln_eps)
    return (centred / spread, spread)


def mini_step(inner_state, batch_block, norm_gain, offset):
    w_first, b_first, w_second, b_second = inner_state
    queries, key_rows, value_rows, lr_rows = batch_block
    mini_len = queries.shape[0]
    hidden_pre = matmul(key_rows, w_first) + b_first
    hidden = gelu_tanh(hidden_pre)
    second = matmul(hidden, w_second) + b_second
    target = value_rows - key_rows
    normed, spread = normalize(second)
    grad_out = norm_gain * (norm_gain * normed + offset - target)
    feat_width = second.shape[-1]
    grad_second = (
        feat_width * grad_out
        - jnp.sum(grad_out, axis=-1, keepdims=True)
        - normed * jnp.sum(grad_out * normed, axis=-1, keepdims=True)
    ) / (feat_width * spread)
    grad_first = matmul(grad_second, w_second.T) * gelu_slope(hidden_pre)
    tri_mask = jnp.tril(jnp.ones((mini_len, mini_len), jnp.float32))
    eta_last = lr_rows / mini_len
    eta_table = tri_mask * eta_last[None, :]
    query_keys = matmul(queries, key_rows.T) * eta_table
    bias_first = b_first - matmul(eta_table, grad_first)
    first_bar = matmul(queries, w_first) - matmul(query_keys, grad_first) + bias_first
    hidden_bar = gelu_tanh(first_bar)
    hidden_pairs = matmul(hidden_bar, hidden.T) * eta_table
    bias_second = b_second - matmul(eta_table, grad_second)
    second_bar = matmul(hidden_bar, w_second) - matmul(hidden_pairs, grad_second) + bias_second
    w_first = w_first - matmul((key_rows * eta_last[:, None]).T, grad_first)
    b_first = b_first - matmul(eta_last[None, :], grad_first)[0]
    w_second = w_second - matmul((hidden * eta_last[:, None]).T, grad_second)
    b_second = b_second - matmul(eta_last[None, :], grad_second)[0]
    normed_bar, spread_bar = normalize(second_bar)
    result = queries + norm_gain * normed_bar + offset
    return ((w_first, b_first, w_second, b_second), result)


def run_blocks(inner_state, queries, key_rows, value_rows, lr_rows, norm_gain, offset, mini_len):
    block_count = queries.shape[0] // mini_len
    blocks = (
        queries.reshape(block_count, mini_len, -1),
        key_rows.reshape(block_count, mini_len, -1),
        value_rows.reshape(block_count, mini_len, -1),
        lr_rows.reshape(block_count, mini_len),
    )

    def advance(loop_carry, batch_block):
        return mini_step(loop_carry, batch_block, norm_gain, offset)

    inner_state, results = lax.scan(advance, inner_state, blocks)
    return (inner_state, results.reshape(queries.shape[0], -1))


def pack_state(state):
    videos = state[0].shape[0]
    return jnp.concatenate([part.reshape(videos, -1) for part in state], axis=1)


def unpack_state(flat, like):
    parts = []
    at = 0
    for part in like:
        width = part[0].size
        parts.append(flat[:, at : at + width].reshape(part.shape))
        at += width
    return tuple(parts)


def exchange_kernel(peer_count, part_ref, recv_ref, send_sems, recv_sems, own_sem):
    me = lax.axis_index("z")
    barrier = pltpu.get_barrier_semaphore()
    for step in range(1, peer_count):
        peer = lax.rem(me + step, peer_count)
        pl.semaphore_signal(barrier, inc=1, device_id={"z": peer}, device_id_type=MESH_ID)
    pl.semaphore_wait(barrier, peer_count - 1)
    own = pltpu.make_async_copy(part_ref.at[me], recv_ref.at[me], own_sem)
    own.start()
    copies = []
    for step in range(1, peer_count):
        peer = lax.rem(me + step, peer_count)
        copy = pltpu.make_async_remote_copy(
            src_ref=part_ref.at[peer],
            dst_ref=recv_ref.at[me],
            send_sem=send_sems.at[step],
            recv_sem=recv_sems.at[step],
            device_id={"z": peer},
            device_id_type=MESH_ID,
        )
        copy.start()
        copies.append(copy)
    for copy in copies:
        copy.wait()
    own.wait()


def exchange_over_z(pieces):
    peer_count = pieces.shape[0]
    moved = pieces.size * pieces.dtype.itemsize
    return pl.pallas_call(
        partial(exchange_kernel, peer_count),
        out_shape=jax.ShapeDtypeStruct(pieces.shape, pieces.dtype),
        in_specs=[pl.BlockSpec(memory_space=pl.ANY)],
        out_specs=pl.BlockSpec(memory_space=pl.ANY),
        scratch_shapes=[
            pltpu.SemaphoreType.DMA((peer_count,)),
            pltpu.SemaphoreType.DMA((peer_count,)),
            pltpu.SemaphoreType.DMA(()),
        ],
        compiler_params=pltpu.CompilerParams(collective_id=0, has_side_effects=True),
        cost_estimate=pl.CostEstimate(flops=0, bytes_accessed=2 * moved, transcendentals=0),
    )(pieces)


def on_device(
    tokens,
    w_qkv,
    w_rate,
    rate_bias,
    w_out,
    w_first_init,
    b_first_init,
    w_second_init,
    b_second_init,
    ln_gain,
    ln_bias,
):
    videos, tok_part, feat_width = tokens.shape
    row_axes = ("xlo", "z", "core")
    pair_axes = ("xlo", "core")
    row_count = lax.axis_size(row_axes)
    z_count = lax.axis_size("z")
    pair_count = lax.axis_size(pair_axes)
    seg_len = tok_part * row_count
    proj_width = w_qkv.shape[0]
    head_size = proj_width // 3
    stacked = jnp.concatenate([w_qkv, w_rate], axis=0)
    gathered = lax.all_gather(tokens, row_axes, axis=1, tiled=True)
    gathered, w_out = lax.optimization_barrier((gathered, w_out))
    w_out_pair = lax.all_gather(w_out, pair_axes, axis=0, tiled=True)
    combined = jnp.einsum(
        "vkd,cd->vkc",
        gathered,
        stacked,
        preferred_element_type=jnp.float32,
    )
    projected = lax.optimization_barrier(combined[:, :, :proj_width].astype(jnp.bfloat16)).astype(
        jnp.float32
    )
    queries = projected[:, :, :head_size]
    key_rows = projected[:, :, head_size : 2 * head_size]
    value_rows = projected[:, :, 2 * head_size :]
    lr_rows = base_rate * jax.nn.sigmoid(combined[:, :, proj_width] + rate_bias[0])
    initial = (w_first_init[0], b_first_init[0], w_second_init[0], b_second_init[0])
    norm_gain = ln_gain[0]
    offset = ln_bias[0]

    def segment(inner_state, video_q, video_k, video_v, video_lr):
        return run_blocks(inner_state, video_q, video_k, video_v, video_lr, norm_gain, offset, MINI)

    seq_count = lax.axis_size("seq")
    seq_place = lax.axis_index("seq")
    first_device = seq_place == 0

    def spread_videos(entries):
        return jnp.broadcast_to(entries, (videos,) + entries.shape)

    start_states = jax.tree.map(spread_videos, initial)
    incoming = start_states
    for turn_idx in range(seq_count):
        finals, results = jax.vmap(segment)(incoming, queries, key_rows, value_rows, lr_rows)
        if turn_idx == 1:
            w_out_pair, finals = lax.optimization_barrier((w_out_pair, finals))
        if turn_idx + 1 < seq_count:
            with jax.named_scope("state_hop"):
                received = unpack_state(passed_along(pack_state(finals), "seq", 1), finals)
            incoming = jax.tree.map(partial(jnp.where, first_device), start_states, received)
    heads_rows = results.astype(jnp.bfloat16)
    with jax.named_scope("output_mix"):
        by_owner = heads_rows.reshape(videos, 2, z_count, 2, tok_part, head_size)
        by_owner = by_owner.transpose(1, 3, 0, 2, 4, 5).reshape(
            pair_count, videos, z_count, tok_part, head_size
        )
        by_head = lax.all_to_all(by_owner, pair_axes, 0, 0, tiled=True)
        partial_terms = jnp.einsum(
            "gvzic,gcd->zvid",
            by_head,
            w_out_pair.reshape(pair_count, head_size, feat_width),
            preferred_element_type=jnp.float32,
        )
        pieces = exchange_over_z(
            partial_terms.reshape(z_count, -1, 1024).astype(jnp.bfloat16)
        )
        mixed_out = jnp.sum(pieces.astype(jnp.float32), axis=0)
    return mixed_out.reshape(videos, tok_part, feat_width).astype(jnp.bfloat16)


def solution(mesh):
    seq_count, row_count = mesh.devices.shape
    fine = jax.sharding.Mesh(
        mesh.devices.reshape(seq_count, 2, row_count // 4, 2), ("seq", "xlo", "z", "core")
    )
    row = ("xlo", "z", "core")
    in_specs = (
        P(None, ("seq",) + row, None),
        P(row, None),
        P(row, None),
        P(row),
        P(row, None),
        P(row, None, None),
        P(row, None),
        P(row, None, None),
        P(row, None),
        P(row, None),
        P(row, None),
    )
    out_specs = P(None, ("seq",) + row, None)
    return jax.shard_map(
        on_device, mesh=fine, in_specs=in_specs, out_specs=out_specs, check_vma=False
    )
```

```python
from functools import partial

import jax
import jax.numpy as jnp
from jax import lax
from jax.experimental import pallas as pl
from jax.experimental.pallas import tpu as pltpu
from jax.sharding import PartitionSpec as P

MESH_ID = pl.DeviceIdType.MESH

MINI = 64


gelu_coef = 0.7978845608028654
base_rate = 0.01
ln_eps = 1e-06


def passed_along(array, axis, by):
    size = lax.axis_size(axis)
    pairs = [(i, i + by) for i in range(size) if 0 <= i + by < size]
    return lax.ppermute(array, axis, pairs)


def gelu_tanh(entries):
    tanh_arg = gelu_coef * (entries + 0.044715 * entries * entries * entries)
    return 0.5 * entries * (1.0 + jnp.tanh(tanh_arg))


def gelu_slope(entries):
    tanh_arg = gelu_coef * (entries + 0.044715 * entries * entries * entries)
    tangent = jnp.tanh(tanh_arg)
    return 0.5 * (1.0 + tangent) + 0.5 * entries * (1.0 - tangent * tangent) * gelu_coef * (
        1.0 + 3.0 * 0.044715 * entries * entries
    )


def matmul(left, right):
    return jnp.dot(left, right, precision=lax.Precision.HIGHEST, preferred_element_type=jnp.float32)


def normalize(entries):
    centred = entries - jnp.mean(entries, axis=-1, keepdims=True)
    spread = jnp.sqrt(jnp.mean(centred * centred, axis=-1, keepdims=True) + ln_eps)
    return (centred / spread, spread)


def mini_step(inner_state, batch_block, norm_gain, offset):
    w_first, b_first, w_second, b_second = inner_state
    queries, key_rows, value_rows, lr_rows = batch_block
    mini_len = queries.shape[0]
    hidden_pre = matmul(key_rows, w_first) + b_first
    hidden = gelu_tanh(hidden_pre)
    second = matmul(hidden, w_second) + b_second
    target = value_rows - key_rows
    normed, spread = normalize(second)
    grad_out = norm_gain * (norm_gain * normed + offset - target)
    feat_width = second.shape[-1]
    grad_second = (
        feat_width * grad_out
        - jnp.sum(grad_out, axis=-1, keepdims=True)
        - normed * jnp.sum(grad_out * normed, axis=-1, keepdims=True)
    ) / (feat_width * spread)
    grad_first = matmul(grad_second, w_second.T) * gelu_slope(hidden_pre)
    tri_mask = jnp.tril(jnp.ones((mini_len, mini_len), jnp.float32))
    eta_last = lr_rows / mini_len
    eta_table = tri_mask * eta_last[None, :]
    query_keys = matmul(queries, key_rows.T) * eta_table
    bias_first = b_first - matmul(eta_table, grad_first)
    first_bar = matmul(queries, w_first) - matmul(query_keys, grad_first) + bias_first
    hidden_bar = gelu_tanh(first_bar)
    hidden_pairs = matmul(hidden_bar, hidden.T) * eta_table
    bias_second = b_second - matmul(eta_table, grad_second)
    second_bar = matmul(hidden_bar, w_second) - matmul(hidden_pairs, grad_second) + bias_second
    w_first = w_first - matmul((key_rows * eta_last[:, None]).T, grad_first)
    b_first = b_first - matmul(eta_last[None, :], grad_first)[0]
    w_second = w_second - matmul((hidden * eta_last[:, None]).T, grad_second)
    b_second = b_second - matmul(eta_last[None, :], grad_second)[0]
    normed_bar, spread_bar = normalize(second_bar)
    result = queries + norm_gain * normed_bar + offset
    return ((w_first, b_first, w_second, b_second), result)


def run_blocks(inner_state, queries, key_rows, value_rows, lr_rows, norm_gain, offset, mini_len):
    block_count = queries.shape[0] // mini_len
    blocks = (
        queries.reshape(block_count, mini_len, -1),
        key_rows.reshape(block_count, mini_len, -1),
        value_rows.reshape(block_count, mini_len, -1),
        lr_rows.reshape(block_count, mini_len),
    )

    def advance(loop_carry, batch_block):
        return mini_step(loop_carry, batch_block, norm_gain, offset)

    inner_state, results = lax.scan(advance, inner_state, blocks)
    return (inner_state, results.reshape(queries.shape[0], -1))


def turn_kernel(
    w1_ref, b1_ref, w2_ref, b2_ref, q_ref, k_ref, v_ref, lrr_ref, lrc_ref, gain_ref, bias_ref,
    w1_out, b1_out, w2_out, b2_out, res_ref,
):
    videos = q_ref.shape[0]
    blocks = q_ref.shape[1] // MINI
    feat = q_ref.shape[2]
    gain = gain_ref[...]
    bias = bias_ref[...]
    lower = lax.broadcasted_iota(jnp.int32, (MINI, MINI), 0) >= lax.broadcasted_iota(
        jnp.int32, (MINI, MINI), 1
    )

    def dot_nt(left, right):
        return lax.dot_general(
            left, right, (((1,), (1,)), ((), ())),
            precision=lax.Precision.HIGHEST, preferred_element_type=jnp.float32,
        )

    def norm_rows(entries):
        centred = entries - jnp.mean(entries, axis=-1, keepdims=True)
        spread = jnp.sqrt(jnp.mean(centred * centred, axis=-1, keepdims=True) + ln_eps)
        return centred / spread, spread

    def one_block(blk, carried):
        start = pl.multiple_of(blk * MINI, MINI)
        span = pl.ds(start, MINI)
        updated = []
        for vid in range(videos):
            w_first, b_first, w_second, b_second = carried[vid]
            queries = q_ref[vid, span, :]
            key_rows = k_ref[vid, span, :]
            value_rows = v_ref[vid, span, :]
            eta_row = lrr_ref[vid, pl.ds(blk, 1), :] / MINI
            eta_col = lrc_ref[vid, span, :] / MINI
            hidden_pre = matmul(key_rows, w_first) + b_first
            hidden = gelu_tanh(hidden_pre)
            second = matmul(hidden, w_second) + b_second
            target = value_rows - key_rows
            normed, spread = norm_rows(second)
            grad_out = gain * (gain * normed + bias - target)
            grad_second = (
                feat * grad_out
                - jnp.sum(grad_out, axis=-1, keepdims=True)
                - normed * jnp.sum(grad_out * normed, axis=-1, keepdims=True)
            ) / (feat * spread)
            grad_first = dot_nt(grad_second, w_second) * gelu_slope(hidden_pre)
            eta_table = jnp.where(lower, eta_row, 0.0)
            query_keys = dot_nt(queries, key_rows) * eta_table
            bias_first = b_first - matmul(eta_table, grad_first)
            first_bar = matmul(queries, w_first) - matmul(query_keys, grad_first) + bias_first
            hidden_bar = gelu_tanh(first_bar)
            hidden_pairs = dot_nt(hidden_bar, hidden) * eta_table
            bias_second = b_second - matmul(eta_table, grad_second)
            second_bar = (
                matmul(hidden_bar, w_second) - matmul(hidden_pairs, grad_second) + bias_second
            )
            w_first = w_first - matmul(jnp.transpose(key_rows * eta_col), grad_first)
            b_first = b_first - jnp.sum(eta_col * grad_first, axis=0, keepdims=True)
            w_second = w_second - matmul(jnp.transpose(hidden * eta_col), grad_second)
            b_second = b_second - jnp.sum(eta_col * grad_second, axis=0, keepdims=True)
            normed_bar, _ = norm_rows(second_bar)
            res_ref[vid, span, :] = queries + gain * normed_bar + bias
            updated.append((w_first, b_first, w_second, b_second))
        return tuple(updated)

    states = tuple(
        (w1_ref[vid], b1_ref[vid], w2_ref[vid], b2_ref[vid]) for vid in range(videos)
    )
    states = lax.fori_loop(0, blocks, one_block, states)
    for vid in range(videos):
        w_first, b_first, w_second, b_second = states[vid]
        w1_out[vid] = w_first
        b1_out[vid] = b_first
        w2_out[vid] = w_second
        b2_out[vid] = b_second


def run_turn(inner_state, queries, key_rows, value_rows, lr_rows, norm_gain, offset):
    w_first, b_first, w_second, b_second = inner_state
    videos, seg_len, feat = queries.shape
    blocks = seg_len // MINI
    hidden_width = w_first.shape[-1]
    state_shapes = (
        jax.ShapeDtypeStruct(w_first.shape, jnp.float32),
        jax.ShapeDtypeStruct((videos, 1, hidden_width), jnp.float32),
        jax.ShapeDtypeStruct(w_second.shape, jnp.float32),
        jax.ShapeDtypeStruct((videos, 1, feat), jnp.float32),
    )
    flops = 2 * videos * blocks * MINI * (10 * MINI * hidden_width + 4 * MINI * feat) * 6
    w1n, b1n, w2n, b2n, results = pl.pallas_call(
        turn_kernel,
        out_shape=state_shapes + (jax.ShapeDtypeStruct(queries.shape, jnp.float32),),
        cost_estimate=pl.CostEstimate(
            flops=flops, bytes_accessed=4 * (4 * queries.size + 4 * w_first.size), transcendentals=0
        ),
    )(
        w_first,
        b_first.reshape(videos, 1, hidden_width),
        w_second,
        b_second.reshape(videos, 1, feat),
        queries,
        key_rows,
        value_rows,
        lr_rows.reshape(videos, blocks, MINI),
        lr_rows.reshape(videos, seg_len, 1),
        norm_gain.reshape(1, feat),
        offset.reshape(1, feat),
    )
    return (w1n, b1n.reshape(videos, hidden_width), w2n, b2n.reshape(videos, feat)), results


def pack_state(state):
    videos = state[0].shape[0]
    return jnp.concatenate([part.reshape(videos, -1) for part in state], axis=1)


def unpack_state(flat, like):
    parts = []
    at = 0
    for part in like:
        width = part[0].size
        parts.append(flat[:, at : at + width].reshape(part.shape))
        at += width
    return tuple(parts)


def exchange_kernel(peer_count, part_ref, recv_ref, send_sems, recv_sems, own_sem):
    me = lax.axis_index("z")
    barrier = pltpu.get_barrier_semaphore()
    for step in range(1, peer_count):
        peer = lax.rem(me + step, peer_count)
        pl.semaphore_signal(barrier, inc=1, device_id={"z": peer}, device_id_type=MESH_ID)
    pl.semaphore_wait(barrier, peer_count - 1)
    own = pltpu.make_async_copy(part_ref.at[me], recv_ref.at[me], own_sem)
    own.start()
    copies = []
    for step in range(1, peer_count):
        peer = lax.rem(me + step, peer_count)
        copy = pltpu.make_async_remote_copy(
            src_ref=part_ref.at[peer],
            dst_ref=recv_ref.at[me],
            send_sem=send_sems.at[step],
            recv_sem=recv_sems.at[step],
            device_id={"z": peer},
            device_id_type=MESH_ID,
        )
        copy.start()
        copies.append(copy)
    for copy in copies:
        copy.wait()
    own.wait()


def exchange_over_z(pieces):
    peer_count = pieces.shape[0]
    moved = pieces.size * pieces.dtype.itemsize
    return pl.pallas_call(
        partial(exchange_kernel, peer_count),
        out_shape=jax.ShapeDtypeStruct(pieces.shape, pieces.dtype),
        in_specs=[pl.BlockSpec(memory_space=pl.ANY)],
        out_specs=pl.BlockSpec(memory_space=pl.ANY),
        scratch_shapes=[
            pltpu.SemaphoreType.DMA((peer_count,)),
            pltpu.SemaphoreType.DMA((peer_count,)),
            pltpu.SemaphoreType.DMA(()),
        ],
        compiler_params=pltpu.CompilerParams(collective_id=0, has_side_effects=True),
        cost_estimate=pl.CostEstimate(flops=0, bytes_accessed=2 * moved, transcendentals=0),
    )(pieces)


def on_device(
    tokens,
    w_qkv,
    w_rate,
    rate_bias,
    w_out,
    w_first_init,
    b_first_init,
    w_second_init,
    b_second_init,
    ln_gain,
    ln_bias,
):
    videos, tok_part, feat_width = tokens.shape
    row_axes = ("xlo", "z", "core")
    pair_axes = ("xlo", "core")
    row_count = lax.axis_size(row_axes)
    z_count = lax.axis_size("z")
    pair_count = lax.axis_size(pair_axes)
    seg_len = tok_part * row_count
    proj_width = w_qkv.shape[0]
    head_size = proj_width // 3
    stacked = jnp.concatenate([w_qkv, w_rate], axis=0)
    gathered = lax.all_gather(tokens, row_axes, axis=1, tiled=True)
    gathered, w_out = lax.optimization_barrier((gathered, w_out))
    w_out_pair = lax.all_gather(w_out, pair_axes, axis=0, tiled=True)
    combined = jnp.einsum(
        "vkd,cd->vkc",
        gathered,
        stacked,
        preferred_element_type=jnp.float32,
    )
    projected = lax.optimization_barrier(combined[:, :, :proj_width].astype(jnp.bfloat16)).astype(
        jnp.float32
    )
    queries = projected[:, :, :head_size]
    key_rows = projected[:, :, head_size : 2 * head_size]
    value_rows = projected[:, :, 2 * head_size :]
    lr_rows = base_rate * jax.nn.sigmoid(combined[:, :, proj_width] + rate_bias[0])
    initial = (w_first_init[0], b_first_init[0], w_second_init[0], b_second_init[0])
    norm_gain = ln_gain[0]
    offset = ln_bias[0]

    def segment(inner_state, video_q, video_k, video_v, video_lr):
        return run_blocks(inner_state, video_q, video_k, video_v, video_lr, norm_gain, offset, MINI)

    seq_count = lax.axis_size("seq")
    seq_place = lax.axis_index("seq")
    first_device = seq_place == 0

    def spread_videos(entries):
        return jnp.broadcast_to(entries, (videos,) + entries.shape)

    start_states = jax.tree.map(spread_videos, initial)
    incoming = start_states
    for turn_idx in range(seq_count):
        finals, results = run_turn(
            incoming, queries, key_rows, value_rows, lr_rows, norm_gain, offset
        )
        if turn_idx == 1:
            w_out_pair, finals = lax.optimization_barrier((w_out_pair, finals))
        if turn_idx + 1 < seq_count:
            with jax.named_scope("state_hop"):
                received = unpack_state(passed_along(pack_state(finals), "seq", 1), finals)
            incoming = jax.tree.map(partial(jnp.where, first_device), start_states, received)
    heads_rows = results.astype(jnp.bfloat16)
    with jax.named_scope("output_mix"):
        by_owner = heads_rows.reshape(videos, 2, z_count, 2, tok_part, head_size)
        by_owner = by_owner.transpose(1, 3, 0, 2, 4, 5).reshape(
            pair_count, videos, z_count, tok_part, head_size
        )
        by_head = lax.all_to_all(by_owner, pair_axes, 0, 0, tiled=True)
        partial_terms = jnp.einsum(
            "gvzic,gcd->zvid",
            by_head,
            w_out_pair.reshape(pair_count, head_size, feat_width),
            preferred_element_type=jnp.float32,
        )
        pieces = exchange_over_z(
            partial_terms.reshape(z_count, -1, 1024).astype(jnp.bfloat16)
        )
        mixed_out = jnp.sum(pieces.astype(jnp.float32), axis=0)
    return mixed_out.reshape(videos, tok_part, feat_width).astype(jnp.bfloat16)


def solution(mesh):
    seq_count, row_count = mesh.devices.shape
    fine = jax.sharding.Mesh(
        mesh.devices.reshape(seq_count, 2, row_count // 4, 2), ("seq", "xlo", "z", "core")
    )
    row = ("xlo", "z", "core")
    in_specs = (
        P(None, ("seq",) + row, None),
        P(row, None),
        P(row, None),
        P(row),
        P(row, None),
        P(row, None, None),
        P(row, None),
        P(row, None, None),
        P(row, None),
        P(row, None),
        P(row, None),
    )
    out_specs = P(None, ("seq",) + row, None)
    return jax.shard_map(
        on_device, mesh=fine, in_specs=in_specs, out_specs=out_specs, check_vma=False
    )
```

```python
from functools import partial

import jax
import jax.numpy as jnp
from jax import lax
from jax.experimental import pallas as pl
from jax.experimental.pallas import tpu as pltpu
from jax.sharding import PartitionSpec as P

MESH_ID = pl.DeviceIdType.MESH

MINI = 64


gelu_coef = 0.7978845608028654
base_rate = 0.01
ln_eps = 1e-06


def passed_along(array, axis, by):
    size = lax.axis_size(axis)
    pairs = [(i, i + by) for i in range(size) if 0 <= i + by < size]
    return lax.ppermute(array, axis, pairs)


def gelu_tanh(entries):
    tanh_arg = gelu_coef * (entries + 0.044715 * entries * entries * entries)
    return 0.5 * entries * (1.0 + jnp.tanh(tanh_arg))


def gelu_slope(entries):
    tanh_arg = gelu_coef * (entries + 0.044715 * entries * entries * entries)
    tangent = jnp.tanh(tanh_arg)
    return 0.5 * (1.0 + tangent) + 0.5 * entries * (1.0 - tangent * tangent) * gelu_coef * (
        1.0 + 3.0 * 0.044715 * entries * entries
    )


def matmul(left, right):
    return jnp.dot(left, right, precision=lax.Precision.HIGHEST, preferred_element_type=jnp.float32)


def normalize(entries):
    centred = entries - jnp.mean(entries, axis=-1, keepdims=True)
    spread = jnp.sqrt(jnp.mean(centred * centred, axis=-1, keepdims=True) + ln_eps)
    return (centred / spread, spread)


def mini_step(inner_state, batch_block, norm_gain, offset):
    w_first, b_first, w_second, b_second = inner_state
    queries, key_rows, value_rows, lr_rows = batch_block
    mini_len = queries.shape[0]
    hidden_pre = matmul(key_rows, w_first) + b_first
    hidden = gelu_tanh(hidden_pre)
    second = matmul(hidden, w_second) + b_second
    target = value_rows - key_rows
    normed, spread = normalize(second)
    grad_out = norm_gain * (norm_gain * normed + offset - target)
    feat_width = second.shape[-1]
    grad_second = (
        feat_width * grad_out
        - jnp.sum(grad_out, axis=-1, keepdims=True)
        - normed * jnp.sum(grad_out * normed, axis=-1, keepdims=True)
    ) / (feat_width * spread)
    grad_first = matmul(grad_second, w_second.T) * gelu_slope(hidden_pre)
    tri_mask = jnp.tril(jnp.ones((mini_len, mini_len), jnp.float32))
    eta_last = lr_rows / mini_len
    eta_table = tri_mask * eta_last[None, :]
    query_keys = matmul(queries, key_rows.T) * eta_table
    bias_first = b_first - matmul(eta_table, grad_first)
    first_bar = matmul(queries, w_first) - matmul(query_keys, grad_first) + bias_first
    hidden_bar = gelu_tanh(first_bar)
    hidden_pairs = matmul(hidden_bar, hidden.T) * eta_table
    bias_second = b_second - matmul(eta_table, grad_second)
    second_bar = matmul(hidden_bar, w_second) - matmul(hidden_pairs, grad_second) + bias_second
    w_first = w_first - matmul((key_rows * eta_last[:, None]).T, grad_first)
    b_first = b_first - matmul(eta_last[None, :], grad_first)[0]
    w_second = w_second - matmul((hidden * eta_last[:, None]).T, grad_second)
    b_second = b_second - matmul(eta_last[None, :], grad_second)[0]
    normed_bar, spread_bar = normalize(second_bar)
    result = queries + norm_gain * normed_bar + offset
    return ((w_first, b_first, w_second, b_second), result)


def run_blocks(inner_state, queries, key_rows, value_rows, lr_rows, norm_gain, offset, mini_len):
    block_count = queries.shape[0] // mini_len
    blocks = (
        queries.reshape(block_count, mini_len, -1),
        key_rows.reshape(block_count, mini_len, -1),
        value_rows.reshape(block_count, mini_len, -1),
        lr_rows.reshape(block_count, mini_len),
    )

    def advance(loop_carry, batch_block):
        return mini_step(loop_carry, batch_block, norm_gain, offset)

    inner_state, results = lax.scan(advance, inner_state, blocks)
    return (inner_state, results.reshape(queries.shape[0], -1))


def pack_state(state):
    videos = state[0].shape[0]
    return jnp.concatenate([part.reshape(videos, -1) for part in state], axis=1)


def unpack_state(flat, like):
    parts = []
    at = 0
    for part in like:
        width = part[0].size
        parts.append(flat[:, at : at + width].reshape(part.shape))
        at += width
    return tuple(parts)


def exchange_kernel(peer_count, part_ref, recv_ref, send_sems, recv_sems, own_sem):
    me = lax.axis_index("z")
    barrier = pltpu.get_barrier_semaphore()
    for step in range(1, peer_count):
        peer = lax.rem(me + step, peer_count)
        pl.semaphore_signal(barrier, inc=1, device_id={"z": peer}, device_id_type=MESH_ID)
    pl.semaphore_wait(barrier, peer_count - 1)
    own = pltpu.make_async_copy(part_ref.at[me], recv_ref.at[me], own_sem)
    own.start()
    copies = []
    for step in range(1, peer_count):
        peer = lax.rem(me + step, peer_count)
        copy = pltpu.make_async_remote_copy(
            src_ref=part_ref.at[peer],
            dst_ref=recv_ref.at[me],
            send_sem=send_sems.at[step],
            recv_sem=recv_sems.at[step],
            device_id={"z": peer},
            device_id_type=MESH_ID,
        )
        copy.start()
        copies.append(copy)
    for copy in copies:
        copy.wait()
    own.wait()


def exchange_over_z(pieces):
    peer_count = pieces.shape[0]
    moved = pieces.size * pieces.dtype.itemsize
    return pl.pallas_call(
        partial(exchange_kernel, peer_count),
        out_shape=jax.ShapeDtypeStruct(pieces.shape, pieces.dtype),
        in_specs=[pl.BlockSpec(memory_space=pl.ANY)],
        out_specs=pl.BlockSpec(memory_space=pl.ANY),
        scratch_shapes=[
            pltpu.SemaphoreType.DMA((peer_count,)),
            pltpu.SemaphoreType.DMA((peer_count,)),
            pltpu.SemaphoreType.DMA(()),
        ],
        compiler_params=pltpu.CompilerParams(collective_id=0, has_side_effects=True),
        cost_estimate=pl.CostEstimate(flops=0, bytes_accessed=2 * moved, transcendentals=0),
    )(pieces)


def on_device(
    tokens,
    w_qkv,
    w_rate,
    rate_bias,
    w_out,
    w_first_init,
    b_first_init,
    w_second_init,
    b_second_init,
    ln_gain,
    ln_bias,
):
    videos, tok_part, feat_width = tokens.shape
    row_axes = ("xlo", "z", "core")
    pair_axes = ("xlo", "core")
    row_count = lax.axis_size(row_axes)
    z_count = lax.axis_size("z")
    pair_count = lax.axis_size(pair_axes)
    seg_len = tok_part * row_count
    proj_width = w_qkv.shape[0]
    head_size = proj_width // 3
    stacked = jnp.concatenate([w_qkv, w_rate], axis=0)
    gathered = lax.all_gather(tokens, "z", axis=1, tiled=True)
    gathered = lax.all_gather(gathered, "xlo", axis=1, tiled=True)
    gathered = lax.all_gather(gathered, "core", axis=1, tiled=True)
    gathered, w_out = lax.optimization_barrier((gathered, w_out))
    w_out_pair = lax.all_gather(w_out, pair_axes, axis=0, tiled=True)
    combined = jnp.einsum(
        "vkd,cd->vkc",
        gathered,
        stacked,
        preferred_element_type=jnp.float32,
    )
    combined = combined.reshape(videos, 2, 2, z_count, tok_part, -1)
    combined = combined.transpose(0, 2, 3, 1, 4, 5).reshape(videos, seg_len, -1)
    projected = lax.optimization_barrier(combined[:, :, :proj_width].astype(jnp.bfloat16)).astype(
        jnp.float32
    )
    queries = projected[:, :, :head_size]
    key_rows = projected[:, :, head_size : 2 * head_size]
    value_rows = projected[:, :, 2 * head_size :]
    lr_rows = base_rate * jax.nn.sigmoid(combined[:, :, proj_width] + rate_bias[0])
    initial = (w_first_init[0], b_first_init[0], w_second_init[0], b_second_init[0])
    norm_gain = ln_gain[0]
    offset = ln_bias[0]

    def segment(inner_state, video_q, video_k, video_v, video_lr):
        return run_blocks(inner_state, video_q, video_k, video_v, video_lr, norm_gain, offset, MINI)

    seq_count = lax.axis_size("seq")
    seq_place = lax.axis_index("seq")
    first_device = seq_place == 0

    def spread_videos(entries):
        return jnp.broadcast_to(entries, (videos,) + entries.shape)

    start_states = jax.tree.map(spread_videos, initial)
    incoming = start_states
    for turn_idx in range(seq_count):
        finals, results = jax.vmap(segment)(incoming, queries, key_rows, value_rows, lr_rows)
        if turn_idx == 1:
            w_out_pair, finals = lax.optimization_barrier((w_out_pair, finals))
        if turn_idx + 1 < seq_count:
            with jax.named_scope("state_hop"):
                received = unpack_state(passed_along(pack_state(finals), "seq", 1), finals)
            incoming = jax.tree.map(partial(jnp.where, first_device), start_states, received)
    heads_rows = results.astype(jnp.bfloat16)
    with jax.named_scope("output_mix"):
        by_owner = heads_rows.reshape(videos, 2, z_count, 2, tok_part, head_size)
        by_owner = by_owner.transpose(1, 3, 0, 2, 4, 5).reshape(
            pair_count, videos, z_count, tok_part, head_size
        )
        by_head = lax.all_to_all(by_owner, pair_axes, 0, 0, tiled=True)
        partial_terms = jnp.einsum(
            "gvzic,gcd->zvid",
            by_head,
            w_out_pair.reshape(pair_count, head_size, feat_width),
            preferred_element_type=jnp.float32,
        )
        pieces = exchange_over_z(
            partial_terms.reshape(z_count, -1, 1024).astype(jnp.bfloat16)
        )
        mixed_out = jnp.sum(pieces.astype(jnp.float32), axis=0)
    return mixed_out.reshape(videos, tok_part, feat_width).astype(jnp.bfloat16)


def solution(mesh):
    seq_count, row_count = mesh.devices.shape
    fine = jax.sharding.Mesh(
        mesh.devices.reshape(seq_count, 2, row_count // 4, 2), ("seq", "xlo", "z", "core")
    )
    row = ("xlo", "z", "core")
    in_specs = (
        P(None, ("seq",) + row, None),
        P(row, None),
        P(row, None),
        P(row),
        P(row, None),
        P(row, None, None),
        P(row, None),
        P(row, None, None),
        P(row, None),
        P(row, None),
        P(row, None),
    )
    out_specs = P(None, ("seq",) + row, None)
    return jax.shard_map(
        on_device, mesh=fine, in_specs=in_specs, out_specs=out_specs, check_vma=False
    )
```

```python
from functools import partial

import jax
import jax.numpy as jnp
from jax import lax
from jax.experimental import pallas as pl
from jax.experimental.pallas import tpu as pltpu
from jax.sharding import PartitionSpec as P

MESH_ID = pl.DeviceIdType.MESH

MINI = 64


gelu_coef = 0.7978845608028654
base_rate = 0.01
ln_eps = 1e-06


def passed_along(array, axis, by):
    size = lax.axis_size(axis)
    pairs = [(i, i + by) for i in range(size) if 0 <= i + by < size]
    return lax.ppermute(array, axis, pairs)


def gelu_tanh(entries):
    tanh_arg = gelu_coef * (entries + 0.044715 * entries * entries * entries)
    return 0.5 * entries * (1.0 + jnp.tanh(tanh_arg))


def gelu_slope(entries):
    tanh_arg = gelu_coef * (entries + 0.044715 * entries * entries * entries)
    tangent = jnp.tanh(tanh_arg)
    return 0.5 * (1.0 + tangent) + 0.5 * entries * (1.0 - tangent * tangent) * gelu_coef * (
        1.0 + 3.0 * 0.044715 * entries * entries
    )


def matmul(left, right):
    return jnp.dot(left, right, precision=lax.Precision.HIGHEST, preferred_element_type=jnp.float32)


def normalize(entries):
    centred = entries - jnp.mean(entries, axis=-1, keepdims=True)
    spread = jnp.sqrt(jnp.mean(centred * centred, axis=-1, keepdims=True) + ln_eps)
    return (centred / spread, spread)


def mini_step(inner_state, batch_block, norm_gain, offset):
    w_first, b_first, w_second, b_second = inner_state
    queries, key_rows, value_rows, lr_rows = batch_block
    mini_len = queries.shape[0]
    hidden_pre = matmul(key_rows, w_first) + b_first
    hidden = gelu_tanh(hidden_pre)
    second = matmul(hidden, w_second) + b_second
    target = value_rows - key_rows
    normed, spread = normalize(second)
    grad_out = norm_gain * (norm_gain * normed + offset - target)
    feat_width = second.shape[-1]
    grad_second = (
        feat_width * grad_out
        - jnp.sum(grad_out, axis=-1, keepdims=True)
        - normed * jnp.sum(grad_out * normed, axis=-1, keepdims=True)
    ) / (feat_width * spread)
    grad_first = matmul(grad_second, w_second.T) * gelu_slope(hidden_pre)
    tri_mask = jnp.tril(jnp.ones((mini_len, mini_len), jnp.float32))
    eta_last = lr_rows / mini_len
    eta_table = tri_mask * eta_last[None, :]
    query_keys = matmul(queries, key_rows.T) * eta_table
    bias_first = b_first - matmul(eta_table, grad_first)
    first_bar = matmul(queries, w_first) - matmul(query_keys, grad_first) + bias_first
    hidden_bar = gelu_tanh(first_bar)
    hidden_pairs = matmul(hidden_bar, hidden.T) * eta_table
    bias_second = b_second - matmul(eta_table, grad_second)
    second_bar = matmul(hidden_bar, w_second) - matmul(hidden_pairs, grad_second) + bias_second
    w_first = w_first - matmul((key_rows * eta_last[:, None]).T, grad_first)
    b_first = b_first - matmul(eta_last[None, :], grad_first)[0]
    w_second = w_second - matmul((hidden * eta_last[:, None]).T, grad_second)
    b_second = b_second - matmul(eta_last[None, :], grad_second)[0]
    normed_bar, spread_bar = normalize(second_bar)
    result = queries + norm_gain * normed_bar + offset
    return ((w_first, b_first, w_second, b_second), result)


def run_blocks(inner_state, queries, key_rows, value_rows, lr_rows, norm_gain, offset, mini_len):
    block_count = queries.shape[0] // mini_len
    blocks = (
        queries.reshape(block_count, mini_len, -1),
        key_rows.reshape(block_count, mini_len, -1),
        value_rows.reshape(block_count, mini_len, -1),
        lr_rows.reshape(block_count, mini_len),
    )

    def advance(loop_carry, batch_block):
        return mini_step(loop_carry, batch_block, norm_gain, offset)

    inner_state, results = lax.scan(advance, inner_state, blocks)
    return (inner_state, results.reshape(queries.shape[0], -1))


def pack_state(state):
    videos = state[0].shape[0]
    return jnp.concatenate([part.reshape(videos, -1) for part in state], axis=1)


def unpack_state(flat, like):
    parts = []
    at = 0
    for part in like:
        width = part[0].size
        parts.append(flat[:, at : at + width].reshape(part.shape))
        at += width
    return tuple(parts)


def exchange_kernel(peer_count, part_ref, recv_ref, send_sems, recv_sems, own_sem):
    me = lax.axis_index("z")
    barrier = pltpu.get_barrier_semaphore()
    for step in range(1, peer_count):
        peer = lax.rem(me + step, peer_count)
        pl.semaphore_signal(barrier, inc=1, device_id={"z": peer}, device_id_type=MESH_ID)
    pl.semaphore_wait(barrier, peer_count - 1)
    own = pltpu.make_async_copy(part_ref.at[me], recv_ref.at[me], own_sem)
    own.start()
    copies = []
    for step in range(1, peer_count):
        peer = lax.rem(me + step, peer_count)
        copy = pltpu.make_async_remote_copy(
            src_ref=part_ref.at[peer],
            dst_ref=recv_ref.at[me],
            send_sem=send_sems.at[step],
            recv_sem=recv_sems.at[step],
            device_id={"z": peer},
            device_id_type=MESH_ID,
        )
        copy.start()
        copies.append(copy)
    for copy in copies:
        copy.wait()
    own.wait()


def exchange_over_z(pieces):
    peer_count = pieces.shape[0]
    moved = pieces.size * pieces.dtype.itemsize
    return pl.pallas_call(
        partial(exchange_kernel, peer_count),
        out_shape=jax.ShapeDtypeStruct(pieces.shape, pieces.dtype),
        in_specs=[pl.BlockSpec(memory_space=pl.ANY)],
        out_specs=pl.BlockSpec(memory_space=pl.ANY),
        scratch_shapes=[
            pltpu.SemaphoreType.DMA((peer_count,)),
            pltpu.SemaphoreType.DMA((peer_count,)),
            pltpu.SemaphoreType.DMA(()),
        ],
        compiler_params=pltpu.CompilerParams(collective_id=0, has_side_effects=True),
        cost_estimate=pl.CostEstimate(flops=0, bytes_accessed=2 * moved, transcendentals=0),
    )(pieces)


def on_device(
    tokens,
    w_qkv,
    w_rate,
    rate_bias,
    w_out,
    w_first_init,
    b_first_init,
    w_second_init,
    b_second_init,
    ln_gain,
    ln_bias,
):
    videos, tok_part, feat_width = tokens.shape
    row_axes = ("xlo", "z", "core")
    pair_axes = ("xlo", "core")
    row_count = lax.axis_size(row_axes)
    z_count = lax.axis_size("z")
    pair_count = lax.axis_size(pair_axes)
    seg_len = tok_part * row_count
    proj_width = w_qkv.shape[0]
    head_size = proj_width // 3
    stacked = jnp.concatenate([w_qkv, w_rate], axis=0)
    gathered = lax.all_gather(tokens, row_axes, axis=1, tiled=True)
    gathered, w_out = lax.optimization_barrier((gathered, w_out))
    w_out_pair = lax.all_gather(w_out, pair_axes, axis=0, tiled=True)
    combined = jnp.einsum(
        "vkd,cd->vkc",
        gathered,
        stacked,
        preferred_element_type=jnp.float32,
    )
    projected = lax.optimization_barrier(combined[:, :, :proj_width].astype(jnp.bfloat16)).astype(
        jnp.float32
    )
    queries = projected[:, :, :head_size]
    key_rows = projected[:, :, head_size : 2 * head_size]
    value_rows = projected[:, :, 2 * head_size :]
    lr_rows = base_rate * jax.nn.sigmoid(combined[:, :, proj_width] + rate_bias[0])
    initial = (w_first_init[0], b_first_init[0], w_second_init[0], b_second_init[0])
    norm_gain = ln_gain[0]
    offset = ln_bias[0]

    def segment(inner_state, video_q, video_k, video_v, video_lr):
        return run_blocks(inner_state, video_q, video_k, video_v, video_lr, norm_gain, offset, MINI)

    seq_count = lax.axis_size("seq")
    seq_place = lax.axis_index("seq")
    first_device = seq_place == 0

    def spread_videos(entries):
        return jnp.broadcast_to(entries, (videos,) + entries.shape)

    start_states = jax.tree.map(spread_videos, initial)
    incoming = start_states
    for turn_idx in range(seq_count):
        finals, results = jax.vmap(segment)(incoming, queries, key_rows, value_rows, lr_rows)
        if turn_idx == 1:
            w_out_pair, finals = lax.optimization_barrier((w_out_pair, finals))
        if turn_idx + 1 < seq_count:
            with jax.named_scope("state_hop"):
                origin = pack_state(start_states)
                change = (pack_state(finals) - origin).astype(jnp.bfloat16)
                moved = passed_along(change, "seq", 1).astype(jnp.float32) + origin
                received = unpack_state(moved, finals)
            incoming = jax.tree.map(partial(jnp.where, first_device), start_states, received)
    heads_rows = results.astype(jnp.bfloat16)
    with jax.named_scope("output_mix"):
        by_owner = heads_rows.reshape(videos, 2, z_count, 2, tok_part, head_size)
        by_owner = by_owner.transpose(1, 3, 0, 2, 4, 5).reshape(
            pair_count, videos, z_count, tok_part, head_size
        )
        by_head = lax.all_to_all(by_owner, pair_axes, 0, 0, tiled=True)
        partial_terms = jnp.einsum(
            "gvzic,gcd->zvid",
            by_head,
            w_out_pair.reshape(pair_count, head_size, feat_width),
            preferred_element_type=jnp.float32,
        )
        pieces = exchange_over_z(
            partial_terms.reshape(z_count, -1, 1024).astype(jnp.bfloat16)
        )
        mixed_out = jnp.sum(pieces.astype(jnp.float32), axis=0)
    return mixed_out.reshape(videos, tok_part, feat_width).astype(jnp.bfloat16)


def solution(mesh):
    seq_count, row_count = mesh.devices.shape
    fine = jax.sharding.Mesh(
        mesh.devices.reshape(seq_count, 2, row_count // 4, 2), ("seq", "xlo", "z", "core")
    )
    row = ("xlo", "z", "core")
    in_specs = (
        P(None, ("seq",) + row, None),
        P(row, None),
        P(row, None),
        P(row),
        P(row, None),
        P(row, None, None),
        P(row, None),
        P(row, None, None),
        P(row, None),
        P(row, None),
        P(row, None),
    )
    out_specs = P(None, ("seq",) + row, None)
    return jax.shard_map(
        on_device, mesh=fine, in_specs=in_specs, out_specs=out_specs, check_vma=False
    )
```

```python
from functools import partial

import jax
import jax.numpy as jnp
from jax import lax
from jax.experimental import pallas as pl
from jax.experimental.pallas import tpu as pltpu
from jax.sharding import PartitionSpec as P

MESH_ID = pl.DeviceIdType.MESH

MINI = 64


gelu_coef = 0.7978845608028654
base_rate = 0.01
ln_eps = 1e-06


def passed_along(array, axis, by):
    size = lax.axis_size(axis)
    pairs = [(i, i + by) for i in range(size) if 0 <= i + by < size]
    return lax.ppermute(array, axis, pairs)


def gelu_tanh(entries):
    tanh_arg = gelu_coef * (entries + 0.044715 * entries * entries * entries)
    return 0.5 * entries * (1.0 + jnp.tanh(tanh_arg))


def gelu_slope(entries):
    tanh_arg = gelu_coef * (entries + 0.044715 * entries * entries * entries)
    tangent = jnp.tanh(tanh_arg)
    return 0.5 * (1.0 + tangent) + 0.5 * entries * (1.0 - tangent * tangent) * gelu_coef * (
        1.0 + 3.0 * 0.044715 * entries * entries
    )


def matmul(left, right):
    return jnp.dot(left, right, precision=lax.Precision.HIGHEST, preferred_element_type=jnp.float32)


def normalize(entries):
    centred = entries - jnp.mean(entries, axis=-1, keepdims=True)
    spread = jnp.sqrt(jnp.mean(centred * centred, axis=-1, keepdims=True) + ln_eps)
    return (centred / spread, spread)


def mini_step(inner_state, batch_block, norm_gain, offset):
    w_first, b_first, w_second, b_second = inner_state
    queries, key_rows, value_rows, lr_rows = batch_block
    mini_len = queries.shape[0]
    hidden_pre = matmul(key_rows, w_first) + b_first
    hidden = gelu_tanh(hidden_pre)
    second = matmul(hidden, w_second) + b_second
    target = value_rows - key_rows
    normed, spread = normalize(second)
    grad_out = norm_gain * (norm_gain * normed + offset - target)
    feat_width = second.shape[-1]
    grad_second = (
        feat_width * grad_out
        - jnp.sum(grad_out, axis=-1, keepdims=True)
        - normed * jnp.sum(grad_out * normed, axis=-1, keepdims=True)
    ) / (feat_width * spread)
    grad_first = matmul(grad_second, w_second.T) * gelu_slope(hidden_pre)
    tri_mask = jnp.tril(jnp.ones((mini_len, mini_len), jnp.float32))
    eta_last = lr_rows / mini_len
    eta_table = tri_mask * eta_last[None, :]
    query_keys = matmul(queries, key_rows.T) * eta_table
    bias_first = b_first - matmul(eta_table, grad_first)
    first_bar = matmul(queries, w_first) - matmul(query_keys, grad_first) + bias_first
    hidden_bar = gelu_tanh(first_bar)
    hidden_pairs = matmul(hidden_bar, hidden.T) * eta_table
    bias_second = b_second - matmul(eta_table, grad_second)
    second_bar = matmul(hidden_bar, w_second) - matmul(hidden_pairs, grad_second) + bias_second
    w_first = w_first - matmul((key_rows * eta_last[:, None]).T, grad_first)
    b_first = b_first - matmul(eta_last[None, :], grad_first)[0]
    w_second = w_second - matmul((hidden * eta_last[:, None]).T, grad_second)
    b_second = b_second - matmul(eta_last[None, :], grad_second)[0]
    normed_bar, spread_bar = normalize(second_bar)
    result = queries + norm_gain * normed_bar + offset
    return ((w_first, b_first, w_second, b_second), result)


def run_blocks(inner_state, queries, key_rows, value_rows, lr_rows, norm_gain, offset, mini_len):
    block_count = queries.shape[0] // mini_len
    blocks = (
        queries.reshape(block_count, mini_len, -1),
        key_rows.reshape(block_count, mini_len, -1),
        value_rows.reshape(block_count, mini_len, -1),
        lr_rows.reshape(block_count, mini_len),
    )

    def advance(loop_carry, batch_block):
        return mini_step(loop_carry, batch_block, norm_gain, offset)

    inner_state, results = lax.scan(advance, inner_state, blocks)
    return (inner_state, results.reshape(queries.shape[0], -1))


def hop_kernel(src_ref, dst_ref, send_sem, recv_sem):
    place = lax.axis_index("seq")
    count = lax.axis_size("seq")
    right = lax.rem(place + 1, count)
    left = lax.rem(place + count - 1, count)
    barrier = pltpu.get_barrier_semaphore()
    pl.semaphore_signal(barrier, inc=1, device_id={"seq": left}, device_id_type=MESH_ID)
    pl.semaphore_wait(barrier, 1)
    copy = pltpu.make_async_remote_copy(
        src_ref=src_ref,
        dst_ref=dst_ref,
        send_sem=send_sem,
        recv_sem=recv_sem,
        device_id={"seq": right},
        device_id_type=MESH_ID,
    )
    copy.start()
    copy.wait()


def hop_to_next(change):
    moved = change.size * change.dtype.itemsize
    return pl.pallas_call(
        hop_kernel,
        out_shape=jax.ShapeDtypeStruct(change.shape, change.dtype),
        in_specs=[pl.BlockSpec(memory_space=pl.ANY)],
        out_specs=pl.BlockSpec(memory_space=pl.ANY),
        scratch_shapes=[pltpu.SemaphoreType.DMA(()), pltpu.SemaphoreType.DMA(())],
        compiler_params=pltpu.CompilerParams(collective_id=1, has_side_effects=True),
        cost_estimate=pl.CostEstimate(flops=0, bytes_accessed=2 * moved, transcendentals=0),
    )(change)


def pack_state(state):
    videos = state[0].shape[0]
    return jnp.concatenate([part.reshape(videos, -1) for part in state], axis=1)


def unpack_state(flat, like):
    parts = []
    at = 0
    for part in like:
        width = part[0].size
        parts.append(flat[:, at : at + width].reshape(part.shape))
        at += width
    return tuple(parts)


def exchange_kernel(peer_count, part_ref, recv_ref, send_sems, recv_sems, own_sem):
    me = lax.axis_index("z")
    barrier = pltpu.get_barrier_semaphore()
    for step in range(1, peer_count):
        peer = lax.rem(me + step, peer_count)
        pl.semaphore_signal(barrier, inc=1, device_id={"z": peer}, device_id_type=MESH_ID)
    pl.semaphore_wait(barrier, peer_count - 1)
    own = pltpu.make_async_copy(part_ref.at[me], recv_ref.at[me], own_sem)
    own.start()
    copies = []
    for step in range(1, peer_count):
        peer = lax.rem(me + step, peer_count)
        copy = pltpu.make_async_remote_copy(
            src_ref=part_ref.at[peer],
            dst_ref=recv_ref.at[me],
            send_sem=send_sems.at[step],
            recv_sem=recv_sems.at[step],
            device_id={"z": peer},
            device_id_type=MESH_ID,
        )
        copy.start()
        copies.append(copy)
    for copy in copies:
        copy.wait()
    own.wait()


def exchange_over_z(pieces):
    peer_count = pieces.shape[0]
    moved = pieces.size * pieces.dtype.itemsize
    return pl.pallas_call(
        partial(exchange_kernel, peer_count),
        out_shape=jax.ShapeDtypeStruct(pieces.shape, pieces.dtype),
        in_specs=[pl.BlockSpec(memory_space=pl.ANY)],
        out_specs=pl.BlockSpec(memory_space=pl.ANY),
        scratch_shapes=[
            pltpu.SemaphoreType.DMA((peer_count,)),
            pltpu.SemaphoreType.DMA((peer_count,)),
            pltpu.SemaphoreType.DMA(()),
        ],
        compiler_params=pltpu.CompilerParams(collective_id=0, has_side_effects=True),
        cost_estimate=pl.CostEstimate(flops=0, bytes_accessed=2 * moved, transcendentals=0),
    )(pieces)


def on_device(
    tokens,
    w_qkv,
    w_rate,
    rate_bias,
    w_out,
    w_first_init,
    b_first_init,
    w_second_init,
    b_second_init,
    ln_gain,
    ln_bias,
):
    videos, tok_part, feat_width = tokens.shape
    row_axes = ("xlo", "z", "core")
    pair_axes = ("xlo", "core")
    row_count = lax.axis_size(row_axes)
    z_count = lax.axis_size("z")
    pair_count = lax.axis_size(pair_axes)
    seg_len = tok_part * row_count
    proj_width = w_qkv.shape[0]
    head_size = proj_width // 3
    stacked = jnp.concatenate([w_qkv, w_rate], axis=0)
    gathered = lax.all_gather(tokens, row_axes, axis=1, tiled=True)
    gathered, w_out = lax.optimization_barrier((gathered, w_out))
    w_out_pair = lax.all_gather(w_out, pair_axes, axis=0, tiled=True)
    combined = jnp.einsum(
        "vkd,cd->vkc",
        gathered,
        stacked,
        preferred_element_type=jnp.float32,
    )
    projected = lax.optimization_barrier(combined[:, :, :proj_width].astype(jnp.bfloat16)).astype(
        jnp.float32
    )
    queries = projected[:, :, :head_size]
    key_rows = projected[:, :, head_size : 2 * head_size]
    value_rows = projected[:, :, 2 * head_size :]
    lr_rows = base_rate * jax.nn.sigmoid(combined[:, :, proj_width] + rate_bias[0])
    initial = (w_first_init[0], b_first_init[0], w_second_init[0], b_second_init[0])
    norm_gain = ln_gain[0]
    offset = ln_bias[0]

    def segment(inner_state, video_q, video_k, video_v, video_lr):
        return run_blocks(inner_state, video_q, video_k, video_v, video_lr, norm_gain, offset, MINI)

    seq_count = lax.axis_size("seq")
    seq_place = lax.axis_index("seq")
    first_device = seq_place == 0

    def spread_videos(entries):
        return jnp.broadcast_to(entries, (videos,) + entries.shape)

    start_states = jax.tree.map(spread_videos, initial)
    incoming = start_states
    for turn_idx in range(seq_count):
        finals, results = jax.vmap(segment)(incoming, queries, key_rows, value_rows, lr_rows)
        if turn_idx == 1:
            w_out_pair, finals = lax.optimization_barrier((w_out_pair, finals))
        if turn_idx + 1 < seq_count:
            with jax.named_scope("state_hop"):
                origin = pack_state(start_states)
                change = (pack_state(finals) - origin).astype(jnp.bfloat16)
                moved = hop_to_next(change).astype(jnp.float32) + origin
                received = unpack_state(moved, finals)
            incoming = jax.tree.map(partial(jnp.where, first_device), start_states, received)
    heads_rows = results.astype(jnp.bfloat16)
    with jax.named_scope("output_mix"):
        by_owner = heads_rows.reshape(videos, 2, z_count, 2, tok_part, head_size)
        by_owner = by_owner.transpose(1, 3, 0, 2, 4, 5).reshape(
            pair_count, videos, z_count, tok_part, head_size
        )
        by_head = lax.all_to_all(by_owner, pair_axes, 0, 0, tiled=True)
        partial_terms = jnp.einsum(
            "gvzic,gcd->zvid",
            by_head,
            w_out_pair.reshape(pair_count, head_size, feat_width),
            preferred_element_type=jnp.float32,
        )
        pieces = exchange_over_z(
            partial_terms.reshape(z_count, -1, 1024).astype(jnp.bfloat16)
        )
        mixed_out = jnp.sum(pieces.astype(jnp.float32), axis=0)
    return mixed_out.reshape(videos, tok_part, feat_width).astype(jnp.bfloat16)


def solution(mesh):
    seq_count, row_count = mesh.devices.shape
    fine = jax.sharding.Mesh(
        mesh.devices.reshape(seq_count, 2, row_count // 4, 2), ("seq", "xlo", "z", "core")
    )
    row = ("xlo", "z", "core")
    in_specs = (
        P(None, ("seq",) + row, None),
        P(row, None),
        P(row, None),
        P(row),
        P(row, None),
        P(row, None, None),
        P(row, None),
        P(row, None, None),
        P(row, None),
        P(row, None),
        P(row, None),
    )
    out_specs = P(None, ("seq",) + row, None)
    return jax.shard_map(
        on_device, mesh=fine, in_specs=in_specs, out_specs=out_specs, check_vma=False
    )
```

```python
from functools import partial

import jax
import jax.numpy as jnp
from jax import lax
from jax.experimental import pallas as pl
from jax.experimental.pallas import tpu as pltpu
from jax.sharding import PartitionSpec as P

MESH_ID = pl.DeviceIdType.MESH

MINI = 64


gelu_coef = 0.7978845608028654
base_rate = 0.01
ln_eps = 1e-06


def passed_along(array, axis, by):
    size = lax.axis_size(axis)
    pairs = [(i, i + by) for i in range(size) if 0 <= i + by < size]
    return lax.ppermute(array, axis, pairs)


def gelu_tanh(entries):
    tanh_arg = gelu_coef * (entries + 0.044715 * entries * entries * entries)
    return 0.5 * entries * (1.0 + jnp.tanh(tanh_arg))


def gelu_slope(entries):
    tanh_arg = gelu_coef * (entries + 0.044715 * entries * entries * entries)
    tangent = jnp.tanh(tanh_arg)
    return 0.5 * (1.0 + tangent) + 0.5 * entries * (1.0 - tangent * tangent) * gelu_coef * (
        1.0 + 3.0 * 0.044715 * entries * entries
    )


def matmul(left, right):
    return jnp.dot(left, right, precision=lax.Precision.HIGHEST, preferred_element_type=jnp.float32)


def normalize(entries):
    centred = entries - jnp.mean(entries, axis=-1, keepdims=True)
    spread = jnp.sqrt(jnp.mean(centred * centred, axis=-1, keepdims=True) + ln_eps)
    return (centred / spread, spread)


def mini_step(inner_state, batch_block, norm_gain, offset):
    w_first, b_first, w_second, b_second = inner_state
    queries, key_rows, value_rows, lr_rows = batch_block
    mini_len = queries.shape[0]
    hidden_pre = matmul(key_rows, w_first) + b_first
    hidden = gelu_tanh(hidden_pre)
    second = matmul(hidden, w_second) + b_second
    target = value_rows - key_rows
    normed, spread = normalize(second)
    grad_out = norm_gain * (norm_gain * normed + offset - target)
    feat_width = second.shape[-1]
    grad_second = (
        feat_width * grad_out
        - jnp.sum(grad_out, axis=-1, keepdims=True)
        - normed * jnp.sum(grad_out * normed, axis=-1, keepdims=True)
    ) / (feat_width * spread)
    grad_first = matmul(grad_second, w_second.T) * gelu_slope(hidden_pre)
    tri_mask = jnp.tril(jnp.ones((mini_len, mini_len), jnp.float32))
    eta_last = lr_rows / mini_len
    eta_table = tri_mask * eta_last[None, :]
    query_keys = matmul(queries, key_rows.T) * eta_table
    bias_first = b_first - matmul(eta_table, grad_first)
    first_bar = matmul(queries, w_first) - matmul(query_keys, grad_first) + bias_first
    hidden_bar = gelu_tanh(first_bar)
    hidden_pairs = matmul(hidden_bar, hidden.T) * eta_table
    bias_second = b_second - matmul(eta_table, grad_second)
    second_bar = matmul(hidden_bar, w_second) - matmul(hidden_pairs, grad_second) + bias_second
    w_first = w_first - matmul((key_rows * eta_last[:, None]).T, grad_first)
    b_first = b_first - matmul(eta_last[None, :], grad_first)[0]
    w_second = w_second - matmul((hidden * eta_last[:, None]).T, grad_second)
    b_second = b_second - matmul(eta_last[None, :], grad_second)[0]
    normed_bar, spread_bar = normalize(second_bar)
    result = queries + norm_gain * normed_bar + offset
    return ((w_first, b_first, w_second, b_second), result)


def run_blocks(inner_state, queries, key_rows, value_rows, lr_rows, norm_gain, offset, mini_len):
    block_count = queries.shape[0] // mini_len
    blocks = (
        queries.reshape(block_count, mini_len, -1),
        key_rows.reshape(block_count, mini_len, -1),
        value_rows.reshape(block_count, mini_len, -1),
        lr_rows.reshape(block_count, mini_len),
    )

    def advance(loop_carry, batch_block):
        return mini_step(loop_carry, batch_block, norm_gain, offset)

    inner_state, results = lax.scan(advance, inner_state, blocks)
    return (inner_state, results.reshape(queries.shape[0], -1))


def pack_state(state):
    videos = state[0].shape[0]
    return jnp.concatenate([part.reshape(videos, -1) for part in state], axis=1)


def unpack_state(flat, like):
    parts = []
    at = 0
    for part in like:
        width = part[0].size
        parts.append(flat[:, at : at + width].reshape(part.shape))
        at += width
    return tuple(parts)


def exchange_kernel(peer_count, part_ref, recv_ref, send_sems, recv_sems, own_sem):
    me = lax.axis_index("z")
    barrier = pltpu.get_barrier_semaphore()
    for step in range(1, peer_count):
        peer = lax.rem(me + step, peer_count)
        pl.semaphore_signal(barrier, inc=1, device_id={"z": peer}, device_id_type=MESH_ID)
    pl.semaphore_wait(barrier, peer_count - 1)
    own = pltpu.make_async_copy(part_ref.at[me], recv_ref.at[me], own_sem)
    own.start()
    copies = []
    for step in range(1, peer_count):
        peer = lax.rem(me + step, peer_count)
        copy = pltpu.make_async_remote_copy(
            src_ref=part_ref.at[peer],
            dst_ref=recv_ref.at[me],
            send_sem=send_sems.at[step],
            recv_sem=recv_sems.at[step],
            device_id={"z": peer},
            device_id_type=MESH_ID,
        )
        copy.start()
        copies.append(copy)
    for copy in copies:
        copy.wait()
    own.wait()


def exchange_over_z(pieces):
    peer_count = pieces.shape[0]
    moved = pieces.size * pieces.dtype.itemsize
    return pl.pallas_call(
        partial(exchange_kernel, peer_count),
        out_shape=jax.ShapeDtypeStruct(pieces.shape, pieces.dtype),
        in_specs=[pl.BlockSpec(memory_space=pl.ANY)],
        out_specs=pl.BlockSpec(memory_space=pl.ANY),
        scratch_shapes=[
            pltpu.SemaphoreType.DMA((peer_count,)),
            pltpu.SemaphoreType.DMA((peer_count,)),
            pltpu.SemaphoreType.DMA(()),
        ],
        compiler_params=pltpu.CompilerParams(collective_id=0, has_side_effects=True),
        cost_estimate=pl.CostEstimate(flops=0, bytes_accessed=2 * moved, transcendentals=0),
    )(pieces)


def on_device(
    tokens,
    w_qkv,
    w_rate,
    rate_bias,
    w_out,
    w_first_init,
    b_first_init,
    w_second_init,
    b_second_init,
    ln_gain,
    ln_bias,
):
    videos, tok_part, feat_width = tokens.shape
    row_axes = ("xlo", "z", "core")
    pair_axes = ("xlo", "core")
    row_count = lax.axis_size(row_axes)
    z_count = lax.axis_size("z")
    pair_count = lax.axis_size(pair_axes)
    seg_len = tok_part * row_count
    proj_width = w_qkv.shape[0]
    head_size = proj_width // 3
    stacked = jnp.concatenate([w_qkv, w_rate], axis=0)
    gathered = lax.all_gather(tokens, row_axes, axis=1, tiled=True)
    gathered, w_out = lax.optimization_barrier((gathered, w_out))
    w_out_pair = lax.all_gather(w_out, pair_axes, axis=0, tiled=True)
    combined = jnp.einsum(
        "vkd,cd->vkc",
        gathered,
        stacked,
        preferred_element_type=jnp.float32,
    )
    projected = lax.optimization_barrier(combined[:, :, :proj_width].astype(jnp.bfloat16)).astype(
        jnp.float32
    )
    queries = projected[:, :, :head_size]
    key_rows = projected[:, :, head_size : 2 * head_size]
    value_rows = projected[:, :, 2 * head_size :]
    lr_rows = base_rate * jax.nn.sigmoid(combined[:, :, proj_width] + rate_bias[0])
    initial = (w_first_init[0], b_first_init[0], w_second_init[0], b_second_init[0])
    norm_gain = ln_gain[0]
    offset = ln_bias[0]

    def segment(inner_state, video_q, video_k, video_v, video_lr):
        return run_blocks(inner_state, video_q, video_k, video_v, video_lr, norm_gain, offset, MINI)

    seq_count = lax.axis_size("seq")
    seq_place = lax.axis_index("seq")
    first_device = seq_place == 0

    def spread_videos(entries):
        return jnp.broadcast_to(entries, (videos,) + entries.shape)

    start_states = jax.tree.map(spread_videos, initial)
    incoming = start_states
    for turn_idx in range(seq_count):
        finals, results = jax.vmap(segment)(incoming, queries, key_rows, value_rows, lr_rows)
        if turn_idx + 1 < seq_count:
            with jax.named_scope("state_hop"):
                origin = pack_state(start_states)
                change = (pack_state(finals) - origin).astype(jnp.bfloat16)
                moved = passed_along(change, "seq", 1).astype(jnp.float32) + origin
                received = unpack_state(moved, finals)
            incoming = jax.tree.map(partial(jnp.where, first_device), start_states, received)
    heads_rows = results.astype(jnp.bfloat16)
    with jax.named_scope("output_mix"):
        by_owner = heads_rows.reshape(videos, 2, z_count, 2, tok_part, head_size)
        by_owner = by_owner.transpose(1, 3, 0, 2, 4, 5).reshape(
            pair_count, videos, z_count, tok_part, head_size
        )
        by_head = lax.all_to_all(by_owner, pair_axes, 0, 0, tiled=True)
        partial_terms = jnp.einsum(
            "gvzic,gcd->zvid",
            by_head,
            w_out_pair.reshape(pair_count, head_size, feat_width),
            preferred_element_type=jnp.float32,
        )
        pieces = exchange_over_z(
            partial_terms.reshape(z_count, -1, 1024).astype(jnp.bfloat16)
        )
        mixed_out = jnp.sum(pieces.astype(jnp.float32), axis=0)
    return mixed_out.reshape(videos, tok_part, feat_width).astype(jnp.bfloat16)


def solution(mesh):
    seq_count, row_count = mesh.devices.shape
    fine = jax.sharding.Mesh(
        mesh.devices.reshape(seq_count, 2, row_count // 4, 2), ("seq", "xlo", "z", "core")
    )
    row = ("xlo", "z", "core")
    in_specs = (
        P(None, ("seq",) + row, None),
        P(row, None),
        P(row, None),
        P(row),
        P(row, None),
        P(row, None, None),
        P(row, None),
        P(row, None, None),
        P(row, None),
        P(row, None),
        P(row, None),
    )
    out_specs = P(None, ("seq",) + row, None)
    return jax.shard_map(
        on_device, mesh=fine, in_specs=in_specs, out_specs=out_specs, check_vma=False
    )
```

```python
from functools import partial

import jax
import jax.numpy as jnp
from jax import lax
from jax.experimental import pallas as pl
from jax.experimental.pallas import tpu as pltpu
from jax.sharding import PartitionSpec as P

MESH_ID = pl.DeviceIdType.MESH

MINI = 64


gelu_coef = 0.7978845608028654
base_rate = 0.01
ln_eps = 1e-06


def passed_along(array, axis, by):
    size = lax.axis_size(axis)
    pairs = [(i, i + by) for i in range(size) if 0 <= i + by < size]
    return lax.ppermute(array, axis, pairs)


def gelu_tanh(entries):
    tanh_arg = gelu_coef * (entries + 0.044715 * entries * entries * entries)
    return 0.5 * entries * (1.0 + jnp.tanh(tanh_arg))


def gelu_slope(entries):
    tanh_arg = gelu_coef * (entries + 0.044715 * entries * entries * entries)
    tangent = jnp.tanh(tanh_arg)
    return 0.5 * (1.0 + tangent) + 0.5 * entries * (1.0 - tangent * tangent) * gelu_coef * (
        1.0 + 3.0 * 0.044715 * entries * entries
    )


def matmul(left, right):
    return jnp.dot(left, right, precision=lax.Precision.HIGHEST, preferred_element_type=jnp.float32)


def normalize(entries):
    centred = entries - jnp.mean(entries, axis=-1, keepdims=True)
    spread = jnp.sqrt(jnp.mean(centred * centred, axis=-1, keepdims=True) + ln_eps)
    return (centred / spread, spread)


def mini_step(inner_state, batch_block, norm_gain, offset):
    w_first, b_first, w_second, b_second = inner_state
    queries, key_rows, value_rows, lr_rows = batch_block
    mini_len = queries.shape[0]
    hidden_pre = matmul(key_rows, w_first) + b_first
    hidden = gelu_tanh(hidden_pre)
    second = matmul(hidden, w_second) + b_second
    target = value_rows - key_rows
    normed, spread = normalize(second)
    grad_out = norm_gain * (norm_gain * normed + offset - target)
    feat_width = second.shape[-1]
    grad_second = (
        feat_width * grad_out
        - jnp.sum(grad_out, axis=-1, keepdims=True)
        - normed * jnp.sum(grad_out * normed, axis=-1, keepdims=True)
    ) / (feat_width * spread)
    grad_first = matmul(grad_second, w_second.T) * gelu_slope(hidden_pre)
    tri_mask = jnp.tril(jnp.ones((mini_len, mini_len), jnp.float32))
    eta_last = lr_rows / mini_len
    eta_table = tri_mask * eta_last[None, :]
    query_keys = matmul(queries, key_rows.T) * eta_table
    bias_first = b_first - matmul(eta_table, grad_first)
    first_bar = matmul(queries, w_first) - matmul(query_keys, grad_first) + bias_first
    hidden_bar = gelu_tanh(first_bar)
    hidden_pairs = matmul(hidden_bar, hidden.T) * eta_table
    bias_second = b_second - matmul(eta_table, grad_second)
    second_bar = matmul(hidden_bar, w_second) - matmul(hidden_pairs, grad_second) + bias_second
    w_first = w_first - matmul((key_rows * eta_last[:, None]).T, grad_first)
    b_first = b_first - matmul(eta_last[None, :], grad_first)[0]
    w_second = w_second - matmul((hidden * eta_last[:, None]).T, grad_second)
    b_second = b_second - matmul(eta_last[None, :], grad_second)[0]
    normed_bar, spread_bar = normalize(second_bar)
    result = queries + norm_gain * normed_bar + offset
    return ((w_first, b_first, w_second, b_second), result)


def run_blocks(inner_state, queries, key_rows, value_rows, lr_rows, norm_gain, offset, mini_len):
    block_count = queries.shape[0] // mini_len
    blocks = (
        queries.reshape(block_count, mini_len, -1),
        key_rows.reshape(block_count, mini_len, -1),
        value_rows.reshape(block_count, mini_len, -1),
        lr_rows.reshape(block_count, mini_len),
    )

    def advance(loop_carry, batch_block):
        return mini_step(loop_carry, batch_block, norm_gain, offset)

    inner_state, results = lax.scan(advance, inner_state, blocks, unroll=True)
    return (inner_state, results.reshape(queries.shape[0], -1))


def pack_state(state):
    videos = state[0].shape[0]
    return jnp.concatenate([part.reshape(videos, -1) for part in state], axis=1)


def unpack_state(flat, like):
    parts = []
    at = 0
    for part in like:
        width = part[0].size
        parts.append(flat[:, at : at + width].reshape(part.shape))
        at += width
    return tuple(parts)


def exchange_kernel(peer_count, part_ref, recv_ref, send_sems, recv_sems, own_sem):
    me = lax.axis_index("z")
    barrier = pltpu.get_barrier_semaphore()
    for step in range(1, peer_count):
        peer = lax.rem(me + step, peer_count)
        pl.semaphore_signal(barrier, inc=1, device_id={"z": peer}, device_id_type=MESH_ID)
    pl.semaphore_wait(barrier, peer_count - 1)
    own = pltpu.make_async_copy(part_ref.at[me], recv_ref.at[me], own_sem)
    own.start()
    copies = []
    for step in range(1, peer_count):
        peer = lax.rem(me + step, peer_count)
        copy = pltpu.make_async_remote_copy(
            src_ref=part_ref.at[peer],
            dst_ref=recv_ref.at[me],
            send_sem=send_sems.at[step],
            recv_sem=recv_sems.at[step],
            device_id={"z": peer},
            device_id_type=MESH_ID,
        )
        copy.start()
        copies.append(copy)
    for copy in copies:
        copy.wait()
    own.wait()


def exchange_over_z(pieces):
    peer_count = pieces.shape[0]
    moved = pieces.size * pieces.dtype.itemsize
    return pl.pallas_call(
        partial(exchange_kernel, peer_count),
        out_shape=jax.ShapeDtypeStruct(pieces.shape, pieces.dtype),
        in_specs=[pl.BlockSpec(memory_space=pl.ANY)],
        out_specs=pl.BlockSpec(memory_space=pl.ANY),
        scratch_shapes=[
            pltpu.SemaphoreType.DMA((peer_count,)),
            pltpu.SemaphoreType.DMA((peer_count,)),
            pltpu.SemaphoreType.DMA(()),
        ],
        compiler_params=pltpu.CompilerParams(collective_id=0, has_side_effects=True),
        cost_estimate=pl.CostEstimate(flops=0, bytes_accessed=2 * moved, transcendentals=0),
    )(pieces)


def on_device(
    tokens,
    w_qkv,
    w_rate,
    rate_bias,
    w_out,
    w_first_init,
    b_first_init,
    w_second_init,
    b_second_init,
    ln_gain,
    ln_bias,
):
    videos, tok_part, feat_width = tokens.shape
    row_axes = ("xlo", "z", "core")
    pair_axes = ("xlo", "core")
    row_count = lax.axis_size(row_axes)
    z_count = lax.axis_size("z")
    pair_count = lax.axis_size(pair_axes)
    seg_len = tok_part * row_count
    proj_width = w_qkv.shape[0]
    head_size = proj_width // 3
    stacked = jnp.concatenate([w_qkv, w_rate], axis=0)
    gathered = lax.all_gather(tokens, row_axes, axis=1, tiled=True)
    gathered, w_out = lax.optimization_barrier((gathered, w_out))
    w_out_pair = lax.all_gather(w_out, pair_axes, axis=0, tiled=True)
    combined = jnp.einsum(
        "vkd,cd->vkc",
        gathered,
        stacked,
        preferred_element_type=jnp.float32,
    )
    projected = lax.optimization_barrier(combined[:, :, :proj_width].astype(jnp.bfloat16)).astype(
        jnp.float32
    )
    queries = projected[:, :, :head_size]
    key_rows = projected[:, :, head_size : 2 * head_size]
    value_rows = projected[:, :, 2 * head_size :]
    lr_rows = base_rate * jax.nn.sigmoid(combined[:, :, proj_width] + rate_bias[0])
    initial = (w_first_init[0], b_first_init[0], w_second_init[0], b_second_init[0])
    norm_gain = ln_gain[0]
    offset = ln_bias[0]

    def segment(inner_state, video_q, video_k, video_v, video_lr):
        return run_blocks(inner_state, video_q, video_k, video_v, video_lr, norm_gain, offset, MINI)

    seq_count = lax.axis_size("seq")
    seq_place = lax.axis_index("seq")
    first_device = seq_place == 0

    def spread_videos(entries):
        return jnp.broadcast_to(entries, (videos,) + entries.shape)

    start_states = jax.tree.map(spread_videos, initial)
    incoming = start_states
    for turn_idx in range(seq_count):
        finals, results = jax.vmap(segment)(incoming, queries, key_rows, value_rows, lr_rows)
        if turn_idx + 1 < seq_count:
            with jax.named_scope("state_hop"):
                origin = pack_state(start_states)
                change = (pack_state(finals) - origin).astype(jnp.bfloat16)
                moved = passed_along(change, "seq", 1).astype(jnp.float32) + origin
                received = unpack_state(moved, finals)
            incoming = jax.tree.map(partial(jnp.where, first_device), start_states, received)
    heads_rows = results.astype(jnp.bfloat16)
    with jax.named_scope("output_mix"):
        by_owner = heads_rows.reshape(videos, 2, z_count, 2, tok_part, head_size)
        by_owner = by_owner.transpose(1, 3, 0, 2, 4, 5).reshape(
            pair_count, videos, z_count, tok_part, head_size
        )
        by_head = lax.all_to_all(by_owner, pair_axes, 0, 0, tiled=True)
        partial_terms = jnp.einsum(
            "gvzic,gcd->zvid",
            by_head,
            w_out_pair.reshape(pair_count, head_size, feat_width),
            preferred_element_type=jnp.float32,
        )
        pieces = exchange_over_z(
            partial_terms.reshape(z_count, -1, 1024).astype(jnp.bfloat16)
        )
        mixed_out = jnp.sum(pieces.astype(jnp.float32), axis=0)
    return mixed_out.reshape(videos, tok_part, feat_width).astype(jnp.bfloat16)


def solution(mesh):
    seq_count, row_count = mesh.devices.shape
    fine = jax.sharding.Mesh(
        mesh.devices.reshape(seq_count, 2, row_count // 4, 2), ("seq", "xlo", "z", "core")
    )
    row = ("xlo", "z", "core")
    in_specs = (
        P(None, ("seq",) + row, None),
        P(row, None),
        P(row, None),
        P(row),
        P(row, None),
        P(row, None, None),
        P(row, None),
        P(row, None, None),
        P(row, None),
        P(row, None),
        P(row, None),
    )
    out_specs = P(None, ("seq",) + row, None)
    return jax.shard_map(
        on_device, mesh=fine, in_specs=in_specs, out_specs=out_specs, check_vma=False
    )
```

```python
from functools import partial

import jax
import jax.numpy as jnp
from jax import lax
from jax.experimental import pallas as pl
from jax.experimental.pallas import tpu as pltpu
from jax.sharding import PartitionSpec as P

MESH_ID = pl.DeviceIdType.MESH

MINI = 64


gelu_coef = 0.7978845608028654
base_rate = 0.01
ln_eps = 1e-06


def passed_along(array, axis, by):
    size = lax.axis_size(axis)
    pairs = [(i, i + by) for i in range(size) if 0 <= i + by < size]
    return lax.ppermute(array, axis, pairs)


def gelu_tanh(entries):
    tanh_arg = gelu_coef * (entries + 0.044715 * entries * entries * entries)
    return 0.5 * entries * (1.0 + jnp.tanh(tanh_arg))


def gelu_slope(entries):
    tanh_arg = gelu_coef * (entries + 0.044715 * entries * entries * entries)
    tangent = jnp.tanh(tanh_arg)
    return 0.5 * (1.0 + tangent) + 0.5 * entries * (1.0 - tangent * tangent) * gelu_coef * (
        1.0 + 3.0 * 0.044715 * entries * entries
    )


def matmul(left, right):
    return jnp.dot(left, right, precision=lax.Precision.HIGHEST, preferred_element_type=jnp.float32)


def normalize(entries):
    centred = entries - jnp.mean(entries, axis=-1, keepdims=True)
    spread = jnp.sqrt(jnp.mean(centred * centred, axis=-1, keepdims=True) + ln_eps)
    return (centred / spread, spread)


def mini_step(inner_state, batch_block, norm_gain, offset):
    w_first, b_first, w_second, b_second = inner_state
    queries, key_rows, value_rows, lr_rows = batch_block
    mini_len = queries.shape[0]
    hidden_pre = matmul(key_rows, w_first) + b_first
    hidden = gelu_tanh(hidden_pre)
    second = matmul(hidden, w_second) + b_second
    target = value_rows - key_rows
    normed, spread = normalize(second)
    grad_out = norm_gain * (norm_gain * normed + offset - target)
    feat_width = second.shape[-1]
    grad_second = (
        feat_width * grad_out
        - jnp.sum(grad_out, axis=-1, keepdims=True)
        - normed * jnp.sum(grad_out * normed, axis=-1, keepdims=True)
    ) / (feat_width * spread)
    grad_first = matmul(grad_second, w_second.T) * gelu_slope(hidden_pre)
    tri_mask = jnp.tril(jnp.ones((mini_len, mini_len), jnp.float32))
    eta_last = lr_rows / mini_len
    eta_table = tri_mask * eta_last[None, :]
    query_keys = matmul(queries, key_rows.T) * eta_table
    bias_first = b_first - matmul(eta_table, grad_first)
    first_bar = matmul(queries, w_first) - matmul(query_keys, grad_first) + bias_first
    hidden_bar = gelu_tanh(first_bar)
    hidden_pairs = matmul(hidden_bar, hidden.T) * eta_table
    bias_second = b_second - matmul(eta_table, grad_second)
    second_bar = matmul(hidden_bar, w_second) - matmul(hidden_pairs, grad_second) + bias_second
    w_first = w_first - matmul((key_rows * eta_last[:, None]).T, grad_first)
    b_first = b_first - matmul(eta_last[None, :], grad_first)[0]
    w_second = w_second - matmul((hidden * eta_last[:, None]).T, grad_second)
    b_second = b_second - matmul(eta_last[None, :], grad_second)[0]
    normed_bar, spread_bar = normalize(second_bar)
    result = queries + norm_gain * normed_bar + offset
    return ((w_first, b_first, w_second, b_second), result)


def run_blocks(inner_state, queries, key_rows, value_rows, lr_rows, norm_gain, offset, mini_len):
    block_count = queries.shape[0] // mini_len
    blocks = (
        queries.reshape(block_count, mini_len, -1),
        key_rows.reshape(block_count, mini_len, -1),
        value_rows.reshape(block_count, mini_len, -1),
        lr_rows.reshape(block_count, mini_len),
    )

    def advance(loop_carry, batch_block):
        return mini_step(loop_carry, batch_block, norm_gain, offset)

    inner_state, results = lax.scan(advance, inner_state, blocks, unroll=2)
    return (inner_state, results.reshape(queries.shape[0], -1))


def pack_state(state):
    videos = state[0].shape[0]
    return jnp.concatenate([part.reshape(videos, -1) for part in state], axis=1)


def unpack_state(flat, like):
    parts = []
    at = 0
    for part in like:
        width = part[0].size
        parts.append(flat[:, at : at + width].reshape(part.shape))
        at += width
    return tuple(parts)


def exchange_kernel(peer_count, part_ref, recv_ref, send_sems, recv_sems, own_sem):
    me = lax.axis_index("z")
    barrier = pltpu.get_barrier_semaphore()
    for step in range(1, peer_count):
        peer = lax.rem(me + step, peer_count)
        pl.semaphore_signal(barrier, inc=1, device_id={"z": peer}, device_id_type=MESH_ID)
    pl.semaphore_wait(barrier, peer_count - 1)
    own = pltpu.make_async_copy(part_ref.at[me], recv_ref.at[me], own_sem)
    own.start()
    copies = []
    for step in range(1, peer_count):
        peer = lax.rem(me + step, peer_count)
        copy = pltpu.make_async_remote_copy(
            src_ref=part_ref.at[peer],
            dst_ref=recv_ref.at[me],
            send_sem=send_sems.at[step],
            recv_sem=recv_sems.at[step],
            device_id={"z": peer},
            device_id_type=MESH_ID,
        )
        copy.start()
        copies.append(copy)
    for copy in copies:
        copy.wait()
    own.wait()


def exchange_over_z(pieces):
    peer_count = pieces.shape[0]
    moved = pieces.size * pieces.dtype.itemsize
    return pl.pallas_call(
        partial(exchange_kernel, peer_count),
        out_shape=jax.ShapeDtypeStruct(pieces.shape, pieces.dtype),
        in_specs=[pl.BlockSpec(memory_space=pl.ANY)],
        out_specs=pl.BlockSpec(memory_space=pl.ANY),
        scratch_shapes=[
            pltpu.SemaphoreType.DMA((peer_count,)),
            pltpu.SemaphoreType.DMA((peer_count,)),
            pltpu.SemaphoreType.DMA(()),
        ],
        compiler_params=pltpu.CompilerParams(collective_id=0, has_side_effects=True),
        cost_estimate=pl.CostEstimate(flops=0, bytes_accessed=2 * moved, transcendentals=0),
    )(pieces)


def on_device(
    tokens,
    w_qkv,
    w_rate,
    rate_bias,
    w_out,
    w_first_init,
    b_first_init,
    w_second_init,
    b_second_init,
    ln_gain,
    ln_bias,
):
    videos, tok_part, feat_width = tokens.shape
    row_axes = ("xlo", "z", "core")
    pair_axes = ("xlo", "core")
    row_count = lax.axis_size(row_axes)
    z_count = lax.axis_size("z")
    pair_count = lax.axis_size(pair_axes)
    seg_len = tok_part * row_count
    proj_width = w_qkv.shape[0]
    head_size = proj_width // 3
    stacked = jnp.concatenate([w_qkv, w_rate], axis=0)
    gathered = lax.all_gather(tokens, row_axes, axis=1, tiled=True)
    gathered, w_out = lax.optimization_barrier((gathered, w_out))
    w_out_pair = lax.all_gather(w_out, pair_axes, axis=0, tiled=True)
    combined = jnp.einsum(
        "vkd,cd->vkc",
        gathered,
        stacked,
        preferred_element_type=jnp.float32,
    )
    projected = lax.optimization_barrier(combined[:, :, :proj_width].astype(jnp.bfloat16)).astype(
        jnp.float32
    )
    queries = projected[:, :, :head_size]
    key_rows = projected[:, :, head_size : 2 * head_size]
    value_rows = projected[:, :, 2 * head_size :]
    lr_rows = base_rate * jax.nn.sigmoid(combined[:, :, proj_width] + rate_bias[0])
    initial = (w_first_init[0], b_first_init[0], w_second_init[0], b_second_init[0])
    norm_gain = ln_gain[0]
    offset = ln_bias[0]

    def segment(inner_state, video_q, video_k, video_v, video_lr):
        return run_blocks(inner_state, video_q, video_k, video_v, video_lr, norm_gain, offset, MINI)

    seq_count = lax.axis_size("seq")
    seq_place = lax.axis_index("seq")
    first_device = seq_place == 0

    def spread_videos(entries):
        return jnp.broadcast_to(entries, (videos,) + entries.shape)

    start_states = jax.tree.map(spread_videos, initial)
    incoming = start_states
    for turn_idx in range(seq_count):
        finals, results = jax.vmap(segment)(incoming, queries, key_rows, value_rows, lr_rows)
        if turn_idx + 1 < seq_count:
            with jax.named_scope("state_hop"):
                origin = pack_state(start_states)
                change = (pack_state(finals) - origin).astype(jnp.bfloat16)
                moved = passed_along(change, "seq", 1).astype(jnp.float32) + origin
                received = unpack_state(moved, finals)
            incoming = jax.tree.map(partial(jnp.where, first_device), start_states, received)
    heads_rows = results.astype(jnp.bfloat16)
    with jax.named_scope("output_mix"):
        by_owner = heads_rows.reshape(videos, 2, z_count, 2, tok_part, head_size)
        by_owner = by_owner.transpose(1, 3, 0, 2, 4, 5).reshape(
            pair_count, videos, z_count, tok_part, head_size
        )
        by_head = lax.all_to_all(by_owner, pair_axes, 0, 0, tiled=True)
        partial_terms = jnp.einsum(
            "gvzic,gcd->zvid",
            by_head,
            w_out_pair.reshape(pair_count, head_size, feat_width),
            preferred_element_type=jnp.float32,
        )
        pieces = exchange_over_z(
            partial_terms.reshape(z_count, -1, 1024).astype(jnp.bfloat16)
        )
        mixed_out = jnp.sum(pieces.astype(jnp.float32), axis=0)
    return mixed_out.reshape(videos, tok_part, feat_width).astype(jnp.bfloat16)


def solution(mesh):
    seq_count, row_count = mesh.devices.shape
    fine = jax.sharding.Mesh(
        mesh.devices.reshape(seq_count, 2, row_count // 4, 2), ("seq", "xlo", "z", "core")
    )
    row = ("xlo", "z", "core")
    in_specs = (
        P(None, ("seq",) + row, None),
        P(row, None),
        P(row, None),
        P(row),
        P(row, None),
        P(row, None, None),
        P(row, None),
        P(row, None, None),
        P(row, None),
        P(row, None),
        P(row, None),
    )
    out_specs = P(None, ("seq",) + row, None)
    return jax.shard_map(
        on_device, mesh=fine, in_specs=in_specs, out_specs=out_specs, check_vma=False
    )
```

```python
from functools import partial

import jax
import jax.numpy as jnp
from jax import lax
from jax.experimental import pallas as pl
from jax.experimental.pallas import tpu as pltpu
from jax.sharding import PartitionSpec as P

MESH_ID = pl.DeviceIdType.MESH

MINI = 64


gelu_coef = 0.7978845608028654
base_rate = 0.01
ln_eps = 1e-06


def passed_along(array, axis, by):
    size = lax.axis_size(axis)
    pairs = [(i, i + by) for i in range(size) if 0 <= i + by < size]
    return lax.ppermute(array, axis, pairs)


def gelu_tanh(entries):
    tanh_arg = gelu_coef * (entries + 0.044715 * entries * entries * entries)
    return 0.5 * entries * (1.0 + jnp.tanh(tanh_arg))


def gelu_slope(entries):
    tanh_arg = gelu_coef * (entries + 0.044715 * entries * entries * entries)
    tangent = jnp.tanh(tanh_arg)
    return 0.5 * (1.0 + tangent) + 0.5 * entries * (1.0 - tangent * tangent) * gelu_coef * (
        1.0 + 3.0 * 0.044715 * entries * entries
    )


def matmul(left, right):
    return jnp.dot(left, right, precision=lax.Precision.HIGHEST, preferred_element_type=jnp.float32)


def normalize(entries):
    centred = entries - jnp.mean(entries, axis=-1, keepdims=True)
    spread = jnp.sqrt(jnp.mean(centred * centred, axis=-1, keepdims=True) + ln_eps)
    return (centred / spread, spread)


def mini_step(inner_state, batch_block, norm_gain, offset):
    w_first, b_first, w_second, b_second = inner_state
    queries, key_rows, value_rows, lr_rows = batch_block
    mini_len = queries.shape[0]
    hidden_pre = matmul(key_rows, w_first) + b_first
    hidden = gelu_tanh(hidden_pre)
    second = matmul(hidden, w_second) + b_second
    target = value_rows - key_rows
    normed, spread = normalize(second)
    grad_out = norm_gain * (norm_gain * normed + offset - target)
    feat_width = second.shape[-1]
    grad_second = (
        feat_width * grad_out
        - jnp.sum(grad_out, axis=-1, keepdims=True)
        - normed * jnp.sum(grad_out * normed, axis=-1, keepdims=True)
    ) / (feat_width * spread)
    grad_first = matmul(grad_second, w_second.T) * gelu_slope(hidden_pre)
    tri_mask = jnp.tril(jnp.ones((mini_len, mini_len), jnp.float32))
    eta_last = lr_rows / mini_len
    eta_table = tri_mask * eta_last[None, :]
    query_keys = matmul(queries, key_rows.T) * eta_table
    bias_first = b_first - matmul(eta_table, grad_first)
    first_bar = matmul(queries, w_first) - matmul(query_keys, grad_first) + bias_first
    hidden_bar = gelu_tanh(first_bar)
    hidden_pairs = matmul(hidden_bar, hidden.T) * eta_table
    bias_second = b_second - matmul(eta_table, grad_second)
    second_bar = matmul(hidden_bar, w_second) - matmul(hidden_pairs, grad_second) + bias_second
    w_first = w_first - matmul((key_rows * eta_last[:, None]).T, grad_first)
    b_first = b_first - matmul(eta_last[None, :], grad_first)[0]
    w_second = w_second - matmul((hidden * eta_last[:, None]).T, grad_second)
    b_second = b_second - matmul(eta_last[None, :], grad_second)[0]
    normed_bar, spread_bar = normalize(second_bar)
    result = queries + norm_gain * normed_bar + offset
    return ((w_first, b_first, w_second, b_second), result)


def run_blocks(inner_state, queries, key_rows, value_rows, lr_rows, norm_gain, offset, mini_len):
    block_count = queries.shape[0] // mini_len
    blocks = (
        queries.reshape(block_count, mini_len, -1),
        key_rows.reshape(block_count, mini_len, -1),
        value_rows.reshape(block_count, mini_len, -1),
        lr_rows.reshape(block_count, mini_len),
    )

    def advance(loop_carry, batch_block):
        return mini_step(loop_carry, batch_block, norm_gain, offset)

    inner_state, results = lax.scan(advance, inner_state, blocks, unroll=True)
    return (inner_state, results.reshape(queries.shape[0], -1))


def pack_state(state):
    videos = state[0].shape[0]
    return jnp.concatenate([part.reshape(videos, -1) for part in state], axis=1)


def unpack_state(flat, like):
    parts = []
    at = 0
    for part in like:
        width = part[0].size
        parts.append(flat[:, at : at + width].reshape(part.shape))
        at += width
    return tuple(parts)


def exchange_kernel(peer_count, part_ref, recv_ref, send_sems, recv_sems):
    me = lax.axis_index("z")
    barrier = pltpu.get_barrier_semaphore()
    for step in range(1, peer_count):
        peer = lax.rem(me + step, peer_count)
        pl.semaphore_signal(barrier, inc=1, device_id={"z": peer}, device_id_type=MESH_ID)
    pl.semaphore_wait(barrier, peer_count - 1)
    copies = []
    for step in range(1, peer_count):
        peer = lax.rem(me + step, peer_count)
        copy = pltpu.make_async_remote_copy(
            src_ref=part_ref.at[peer],
            dst_ref=recv_ref.at[me],
            send_sem=send_sems.at[step],
            recv_sem=recv_sems.at[step],
            device_id={"z": peer},
            device_id_type=MESH_ID,
        )
        copy.start()
        copies.append(copy)
    for copy in copies:
        copy.wait()


def exchange_over_z(pieces):
    peer_count = pieces.shape[0]
    moved = pieces.size * pieces.dtype.itemsize
    return pl.pallas_call(
        partial(exchange_kernel, peer_count),
        out_shape=jax.ShapeDtypeStruct(pieces.shape, pieces.dtype),
        in_specs=[pl.BlockSpec(memory_space=pl.ANY)],
        out_specs=pl.BlockSpec(memory_space=pl.ANY),
        scratch_shapes=[
            pltpu.SemaphoreType.DMA((peer_count,)),
            pltpu.SemaphoreType.DMA((peer_count,)),
        ],
        compiler_params=pltpu.CompilerParams(collective_id=0, has_side_effects=True),
        cost_estimate=pl.CostEstimate(flops=0, bytes_accessed=2 * moved, transcendentals=0),
    )(pieces)


def on_device(
    tokens,
    w_qkv,
    w_rate,
    rate_bias,
    w_out,
    w_first_init,
    b_first_init,
    w_second_init,
    b_second_init,
    ln_gain,
    ln_bias,
):
    videos, tok_part, feat_width = tokens.shape
    row_axes = ("xlo", "z", "core")
    pair_axes = ("xlo", "core")
    row_count = lax.axis_size(row_axes)
    z_count = lax.axis_size("z")
    pair_count = lax.axis_size(pair_axes)
    seg_len = tok_part * row_count
    proj_width = w_qkv.shape[0]
    head_size = proj_width // 3
    stacked = jnp.concatenate([w_qkv, w_rate], axis=0)
    gathered = lax.all_gather(tokens, row_axes, axis=1, tiled=True)
    gathered, w_out = lax.optimization_barrier((gathered, w_out))
    w_out_pair = lax.all_gather(w_out, pair_axes, axis=0, tiled=True)
    combined = jnp.einsum(
        "vkd,cd->vkc",
        gathered,
        stacked,
        preferred_element_type=jnp.float32,
    )
    projected = lax.optimization_barrier(combined[:, :, :proj_width].astype(jnp.bfloat16)).astype(
        jnp.float32
    )
    queries = projected[:, :, :head_size]
    key_rows = projected[:, :, head_size : 2 * head_size]
    value_rows = projected[:, :, 2 * head_size :]
    lr_rows = base_rate * jax.nn.sigmoid(combined[:, :, proj_width] + rate_bias[0])
    initial = (w_first_init[0], b_first_init[0], w_second_init[0], b_second_init[0])
    norm_gain = ln_gain[0]
    offset = ln_bias[0]

    def segment(inner_state, video_q, video_k, video_v, video_lr):
        return run_blocks(inner_state, video_q, video_k, video_v, video_lr, norm_gain, offset, MINI)

    seq_count = lax.axis_size("seq")
    seq_place = lax.axis_index("seq")
    first_device = seq_place == 0

    def spread_videos(entries):
        return jnp.broadcast_to(entries, (videos,) + entries.shape)

    start_states = jax.tree.map(spread_videos, initial)
    incoming = start_states
    for turn_idx in range(seq_count):
        finals, results = jax.vmap(segment)(incoming, queries, key_rows, value_rows, lr_rows)
        if turn_idx + 1 < seq_count:
            with jax.named_scope("state_hop"):
                origin = pack_state(start_states)
                change = (pack_state(finals) - origin).astype(jnp.bfloat16)
                moved = passed_along(change, "seq", 1).astype(jnp.float32) + origin
                received = unpack_state(moved, finals)
            incoming = jax.tree.map(partial(jnp.where, first_device), start_states, received)
    heads_rows = results.astype(jnp.bfloat16)
    with jax.named_scope("output_mix"):
        by_owner = heads_rows.reshape(videos, 2, z_count, 2, tok_part, head_size)
        by_owner = by_owner.transpose(1, 3, 0, 2, 4, 5).reshape(
            pair_count, videos, z_count, tok_part, head_size
        )
        by_head = lax.all_to_all(by_owner, pair_axes, 0, 0, tiled=True)
        partial_terms = jnp.einsum(
            "gvzic,gcd->zvid",
            by_head,
            w_out_pair.reshape(pair_count, head_size, feat_width),
            preferred_element_type=jnp.float32,
        )
        pieces = exchange_over_z(
            partial_terms.reshape(z_count, -1, 1024).astype(jnp.bfloat16)
        )
        own_slot = lax.broadcasted_iota(jnp.int32, pieces.shape, 0) == lax.axis_index("z")
        sent = partial_terms.reshape(pieces.shape).astype(jnp.bfloat16)
        mixed_out = jnp.sum(jnp.where(own_slot, sent, pieces).astype(jnp.float32), axis=0)
    return mixed_out.reshape(videos, tok_part, feat_width).astype(jnp.bfloat16)


def solution(mesh):
    seq_count, row_count = mesh.devices.shape
    fine = jax.sharding.Mesh(
        mesh.devices.reshape(seq_count, 2, row_count // 4, 2), ("seq", "xlo", "z", "core")
    )
    row = ("xlo", "z", "core")
    in_specs = (
        P(None, ("seq",) + row, None),
        P(row, None),
        P(row, None),
        P(row),
        P(row, None),
        P(row, None, None),
        P(row, None),
        P(row, None, None),
        P(row, None),
        P(row, None),
        P(row, None),
    )
    out_specs = P(None, ("seq",) + row, None)
    return jax.shard_map(
        on_device, mesh=fine, in_specs=in_specs, out_specs=out_specs, check_vma=False
    )
```
